32 devices in a mesh: row: 2 (over core), col: 16 (over z, y, x).
Axes of the slice: x: 2, y: 2, z: 4, core: 2. Of those that a mesh axis runs over, the one named last changes fastest.
Arguments:
- source_bytes: int32 [2, 2048], P('row', 'col'), may hold values from 0 to 383
- decoder_bytes: int32 [2, 2048], P('row', 'col'), may hold values from 0 to 383
- target_bytes: int32 [2, 2048], P('row', 'col'), may hold values from 0 to 383
- target_keep: int32 [2, 2048], P('row', 'col'), may hold values 0 or 1
- source_length: int32 [2], P('row'), may hold values from 1024 to 2048, as said below
- target_length: int32 [2], P('row'), may hold values from 1024 to 2048, as said below
- language: int32 [2], P('row'), may hold values from 0 to 3, as said below
- step_count: int32 [1], replicated, may hold values from 2 to 20
- attn_weights: float32 [3, 4, 1472, 384], P(None, None, 'row', 'col')
- attn_first: float32 [3, 4, 1472, 384], P(None, None, 'row', 'col'), may hold values from -2.3841858e-06 to 2.3841858e-06
- attn_second: float32 [3, 4, 1472, 384], P(None, None, 'row', 'col'), may hold values from 1.2633388e-15 to 2.0213421e-14
- feed_weights: float32 [2, 3, 16, 329728], P(None, None, 'col', 'row'), may hold values from -0.15625 to 0.15625
- feed_first: float32 [2, 3, 16, 329728], P(None, None, 'col', 'row'), may hold values from -2.3841858e-06 to 2.3841858e-06
- feed_second: float32 [2, 3, 16, 329728], P(None, None, 'col', 'row'), may hold values from 1.2633388e-15 to 2.0213421e-14
- table_weights: float32 [2, 1472, 384], P(None, 'row', 'col')
- table_first: float32 [2, 1472, 384], P(None, 'row', 'col'), may hold values from -2.3841858e-06 to 2.3841858e-06
- table_second: float32 [2, 1472, 384], P(None, 'row', 'col'), may hold values from 1.2633388e-15 to 2.0213421e-14
- norm_gain_stack: float32 [7, 1472], replicated, may hold values from 0.5 to 1.5
- gain_first: float32 [7, 1472], replicated, may hold values from -1.335144e-05 to 1.335144e-05
- gain_second: float32 [7, 1472], replicated, may hold values from 3.158347e-14 to 5.053355e-13
Outputs:
- loss: float32 [], replicated
- grad_norm: float32 [], replicated
- first_attn: float32 [3, 4, 1472, 384], P(None, None, 'row', 'col')
- second_attn: float32 [3, 4, 1472, 384], P(None, None, 'row', 'col')
- master_attn: float32 [3, 4, 1472, 384], P(None, None, 'row', 'col')
- first_feed: float32 [2, 3, 16, 329728], P(None, None, 'col', 'row')
- second_feed: float32 [2, 3, 16, 329728], P(None, None, 'col', 'row')
- master_feed: float32 [2, 3, 16, 329728], P(None, None, 'col', 'row')
- first_table: float32 [2, 1472, 384], P(None, 'row', 'col')
- second_table: float32 [2, 1472, 384], P(None, 'row', 'col')
- master_table: float32 [2, 1472, 384], P(None, 'row', 'col')
- first_gain: float32 [7, 1472], replicated
- second_gain: float32 [7, 1472], replicated
- master_gain: float32 [7, 1472], replicated
The draws below stay inside these ranges and needn't reach their ends.
Inputs may be any that keep to these rules, and one draw needn't show every extreme that they name: `source_length`: one sequence, which one drawn from the seed, fills all 2048 slots; the others hold 1024 or more. `target_length`: one sequence, which one drawn from the seed, fills all 2048 slots; the others hold 1024 or more. `language`: neighbouring sequences belong to different groups; with 4 or more sequences every group occurs.
All inputs are finite; a program needn't handle non-finite values. No bound on the sum of `target_keep` on one device may be relied on, other than what follows from the above.
Results may differ from the reference program's by a relative error of at most 0.012.
The reference program's roundings to bfloat16 on the way count: a program that leaves them out, or rounds other values in their place, can miss the bound.
Values may be sent and summed in bfloat16 or wider, within the bound.
No kernel may reach another device: no remote copies, remote signals or barrier semaphores. Data moves between devices by JAX's collectives and lax.ppermute only.
A program may use at most 384 MiB of HBM per device.

```python
import math
import jax
import jax.numpy as jnp
from jax import lax

D = 1472
HEADS = 6
HEAD_DIM = 64
FF = 3584
VOCAB = 384
NLANG = 4
INNER = 384
SLOT = 2048
SEQS = 2
PARAMS = 39577664
N_COL = 16


def base_normal(key, shape):
    values = jax.random.normal(key, shape, jnp.float32)
    return jnp.clip(values, -6.0, 6.0)


def draw_attn_weights(key, part):
    values = base_normal(jax.random.fold_in(key, 11), (3, 4, D, INNER))
    inner_scale = D ** (-0.5)
    outer_scale = (SLOT / (3.0 * INNER)) ** 0.5
    scales = jnp.array([inner_scale, inner_scale, inner_scale, outer_scale], jnp.float32)
    return values * scales[None, :, None, None]


def draw_table_weights(key, part):
    values = base_normal(jax.random.fold_in(key, 13), (2, D, VOCAB))
    scales = jnp.array([1.0, 1.5 * D ** (-0.5)], jnp.float32)
    return values * scales[:, None, None]


def ragged_lengths(key):
    drawn = jax.random.randint(jax.random.fold_in(key, 1), (SEQS,), SLOT // 2, SLOT + 1)
    full_seq = jax.random.randint(jax.random.fold_in(key, 2), (), 0, SEQS)
    seq_ids = jnp.arange(SEQS, dtype=jnp.int32)
    return jnp.where(seq_ids == full_seq, SLOT, drawn).astype(jnp.int32)


def draw_source_length(key, part):
    return ragged_lengths(jax.random.fold_in(key, 17))


def draw_target_length(key, part):
    return ragged_lengths(jax.random.fold_in(key, 19))


def draw_language(key, part):
    order = jax.random.permutation(jax.random.fold_in(key, 23), NLANG)
    seq_ids = jnp.arange(SEQS, dtype=jnp.int32) % NLANG
    return order[seq_ids].astype(jnp.int32)


def place_ends(values, own_key, low, high):
    index_at = [jax.random.randint(jax.random.fold_in(own_key, axis), (), 0, length) for axis, length in enumerate(values.shape)]
    longest = values.shape.index(max(values.shape))
    beside = index_at[:longest] + [(index_at[longest] + 1) % values.shape[longest]] + index_at[longest + 1:]
    return values.at[tuple(index_at)].set(low).at[tuple(beside)].set(high)


def block_levels(stream_key, dims, shards, least, top_value):
    level, own = 1.0, jax.random.fold_in(stream_key, 6)
    for position, blocks in shards:
        steps = jnp.exp(jax.random.uniform(jax.random.fold_in(own, position), (blocks,), jnp.float32, least / len(shards), top_value / len(shards)))
        level = level * jnp.repeat(steps, dims[position] // blocks).reshape([-1 if axis == position else 1 for axis in range(len(dims))])
    return level


def normal_values(rng, dims, scale, most, cuts=(), kind=jnp.bfloat16):
    values = jax.random.normal(rng, dims, jnp.float32) * scale
    if len(cuts) > 0:
        values = block_levels(rng, dims, cuts, -0.22, 0.18) * values
    return jnp.clip(values, min=-most, max=most).astype(kind)


def setup_inputs(seed: int = 0) -> dict:
    key_of = jax.random.split(jax.random.key(seed), 21)
    source_bytes = place_ends(jax.random.randint(key_of[0], (SEQS, SLOT), 0, VOCAB), jax.random.fold_in(key_of[0], 1), 0, VOCAB - 1).astype(jnp.int32)
    decoder_bytes = place_ends(jax.random.randint(key_of[1], (SEQS, SLOT), 0, VOCAB), jax.random.fold_in(key_of[1], 1), 0, VOCAB - 1).astype(jnp.int32)
    target_bytes = place_ends(jax.random.randint(key_of[2], (SEQS, SLOT), 0, VOCAB), jax.random.fold_in(key_of[2], 1), 0, VOCAB - 1).astype(jnp.int32)
    target_keep = place_ends((jax.random.randint(key_of[3], (SEQS, SLOT), 0, 8) < 7).astype(jnp.int32), jax.random.fold_in(key_of[3], 1), 0, 1)
    source_length = draw_source_length(jax.random.fold_in(key_of[20], 71), 0)
    target_length = draw_target_length(jax.random.fold_in(key_of[20], 71), 0)
    language = draw_language(jax.random.fold_in(key_of[20], 71), 0)
    step_count = jax.random.randint(key_of[7], (1,), 2, 21).astype(jnp.int32)
    attn_weights = draw_attn_weights(jax.random.fold_in(key_of[20], 71), 0)
    attn_first = normal_values(key_of[9], (3, 4, D, INNER), (0.11 * 0.01 / PARAMS ** 0.5), 2.384185791015625e-06, ((2, 2), (3, 16)), jnp.float32)
    attn_second = jnp.clip(jnp.exp(math.log(2.0213421458555383e-14) - 2.7725887 * jax.random.uniform(key_of[10], (3, 4, D, INNER), jnp.float32) ** block_levels(key_of[10], (3, 4, D, INNER), ((2, 2), (3, 16)), -0.2, 0.2)), 1.2633388411597115e-15, 2.0213421458555383e-14)
    feed_weights = normal_values(key_of[11], (2, 3, N_COL, D * (FF // N_COL)), D ** -0.5, 0.15625, ((2, 16), (3, 2)), jnp.float32)
    feed_first = normal_values(key_of[12], (2, 3, N_COL, D * (FF // N_COL)), (0.11 * 0.01 / PARAMS ** 0.5), 2.384185791015625e-06, ((2, 16), (3, 2)), jnp.float32)
    feed_second = jnp.clip(jnp.exp(math.log(2.0213421458555383e-14) - 2.7725887 * jax.random.uniform(key_of[13], (2, 3, N_COL, D * (FF // N_COL)), jnp.float32) ** block_levels(key_of[13], (2, 3, N_COL, D * (FF // N_COL)), ((2, 16), (3, 2)), -0.2, 0.2)), 1.2633388411597115e-15, 2.0213421458555383e-14)
    table_weights = draw_table_weights(jax.random.fold_in(key_of[20], 71), 0)
    table_first = normal_values(key_of[15], (2, D, VOCAB), (0.11 * 0.01 / PARAMS ** 0.5), 2.384185791015625e-06, ((1, 2), (2, 16)), jnp.float32)
    table_second = jnp.clip(jnp.exp(math.log(2.0213421458555383e-14) - 2.7725887 * jax.random.uniform(key_of[16], (2, D, VOCAB), jnp.float32) ** block_levels(key_of[16], (2, D, VOCAB), ((1, 2), (2, 16)), -0.2, 0.2)), 1.2633388411597115e-15, 2.0213421458555383e-14)
    norm_gain_stack = jnp.clip(1.0 + 0.1 * jax.random.normal(key_of[17], (7, D), jnp.float32), 0.5, 1.5)
    gain_first = normal_values(key_of[18], (7, D), (0.55 * 0.01 / PARAMS ** 0.5), 1.33514404296875e-05, (), jnp.float32)
    gain_second = jnp.clip(jnp.exp(jax.random.uniform(key_of[19], (7, D), jnp.float32, math.log(3.15834699702016e-14), math.log(5.053355195232256e-13))), 3.15834699702016e-14, 5.053355195232256e-13)
    return dict(source_bytes=source_bytes, decoder_bytes=decoder_bytes, target_bytes=target_bytes, target_keep=target_keep, source_length=source_length, target_length=target_length, language=language, step_count=step_count, attn_weights=attn_weights, attn_first=attn_first, attn_second=attn_second, feed_weights=feed_weights, feed_first=feed_first, feed_second=feed_second, table_weights=table_weights, table_first=table_first, table_second=table_second, norm_gain_stack=norm_gain_stack, gain_first=gain_first, gain_second=gain_second)


RMS_EPS = 1e-06
CLIP_NORM = 0.01
BETA_FIRST = 0.9
BETA_SECOND = 0.999
ADAM_EPS = 1e-08
MATRIX_RATE = 0.05
GAIN_RATE = 0.2
DECAY_STEP = 0.005
MASKED = -1000000000.0
PRECISE = lax.Precision.HIGHEST

@jax.custom_vjp
def low(v):
    return lax.optimization_barrier(v.astype(jnp.bfloat16)).astype(jnp.float32)

@jax.custom_vjp
def low_back(v):
    return v

def low_keep(v):
    return (low(v), None)

def low_pass(kept, grad):
    return (grad,)

def back_keep(v):
    return (v, None)

def back_low(kept, grad):
    return (low(grad),)
low.defvjp(low_keep, low_pass)
low_back.defvjp(back_keep, back_low)

def rounded(value):
    return low_back(low(value))

def product(left, right):
    return jnp.dot(left, right, precision=PRECISE, preferred_element_type=jnp.float32)

def to_matrix(stored):
    split = stored.reshape(2, 3, N_COL, D, FF // N_COL)
    return split.transpose(0, 1, 3, 2, 4).reshape(2, 3, D, FF)

def from_matrix(matrix):
    split = matrix.reshape(2, 3, D, N_COL, FF // N_COL)
    return split.transpose(0, 1, 3, 2, 4).reshape(2, 3, N_COL, D * (FF // N_COL))

def rms_norm(stream, gain):
    return stream * lax.rsqrt(lax.optimization_barrier(jnp.mean(stream * stream, axis=-1, keepdims=True)) + RMS_EPS) * gain

def score_block(queries, first, key_rows, value_rows, key_limit, causal):
    count = queries.shape[0]
    split_q = queries.reshape(count, HEADS, HEAD_DIM)
    split_k = key_rows.reshape(-1, HEADS, HEAD_DIM)
    split_v = value_rows.reshape(-1, HEADS, HEAD_DIM)
    scores = low_back(jnp.einsum('qhd,khd->hqk', split_q, split_k, precision=PRECISE) * HEAD_DIM ** (-0.5))
    key_pos = jnp.arange(split_k.shape[0], dtype=jnp.int32)
    query_pos = first + jnp.arange(count, dtype=jnp.int32)
    allowed = jnp.broadcast_to(key_pos[None, :] < key_limit, (count, split_k.shape[0]))
    if causal:
        allowed = allowed & (key_pos[None, :] <= query_pos[:, None])
    scores = jnp.where(allowed[None], scores, MASKED)
    probs = jax.nn.softmax(scores, axis=-1)
    context = jnp.einsum('hqk,khd->qhd', low(probs), split_v, precision=PRECISE)
    return context.reshape(count, INNER)

def attend(normed_q, normed_kv, weight_bundle, key_limit, causal):
    queries = rounded(product(normed_q, weight_bundle[0]))
    key_rows = rounded(product(normed_kv, weight_bundle[1]))
    value_rows = rounded(product(normed_kv, weight_bundle[2]))
    length = queries.shape[0]
    block = min(512, length)
    starts = jnp.arange(length // block, dtype=jnp.int32) * block
    blocked = queries.reshape(length // block, block, INNER)
    block_fn = jax.checkpoint(lambda pair: score_block(pair[0], pair[1], key_rows, value_rows, key_limit, causal))
    context = rounded(lax.map(block_fn, (blocked, starts)).reshape(length, INNER))
    return low_back(product(context, weight_bundle[3].T))

def feed_forward(normed, weight_bundle):
    gate = low_back(product(normed, weight_bundle[0]))
    upper = low_back(product(normed, weight_bundle[1]))
    hidden = low(jax.nn.gelu(gate, approximate=True) * upper)
    return low_back(product(hidden, weight_bundle[2].T))

def sequence_loss(attn_b, feed_b, table_b, gains, item):
    source, decoder_in, target, scale, source_limit, target_limit = item
    embed = table_b[0].T
    encoder_layer_zero = embed[source]
    normed = low(rms_norm(encoder_layer_zero, gains[0]))
    enc_one = encoder_layer_zero + attend(normed, normed, attn_b[0], source_limit, False)
    enc_two = enc_one + feed_forward(low(rms_norm(enc_one, gains[1])), feed_b[0])
    memory = low(rms_norm(enc_two, gains[2]))
    decoder_layer_zero = embed[decoder_in]
    normed = low(rms_norm(decoder_layer_zero, gains[3]))
    dec_one = decoder_layer_zero + attend(normed, normed, attn_b[1], target_limit, True)
    dec_two = dec_one + attend(low(rms_norm(dec_one, gains[4])), memory, attn_b[2], source_limit, False)
    dec_three = dec_two + feed_forward(low(rms_norm(dec_two, gains[5])), feed_b[1])
    final = low(rms_norm(dec_three, gains[6]))
    logits = low_back(product(final, table_b[1]))
    lse = jax.nn.logsumexp(logits, axis=-1)
    picked = jnp.take_along_axis(logits, target[:, None], axis=1)[:, 0]
    return jnp.sum((lse - picked) * scale)

def adam(weight_bundle, first, second, grad, clip, count, rate, decay_step):
    clipped = grad * clip
    first_new = BETA_FIRST * first + (1.0 - BETA_FIRST) * clipped
    second_new = BETA_SECOND * second + (1.0 - BETA_SECOND) * clipped * clipped
    fixed_first = first_new / (1.0 - BETA_FIRST ** count)
    fixed_second = second_new / (1.0 - BETA_SECOND ** count)
    master = weight_bundle - rate * (fixed_first / (jnp.sqrt(fixed_second) + ADAM_EPS)) - decay_step * weight_bundle
    return (first_new, second_new, master)

def reference(source_bytes, decoder_bytes, target_bytes, target_keep, source_length, target_length, language, step_count, attn_weights, attn_first, attn_second, feed_weights, feed_first, feed_second, table_weights, table_first, table_second, norm_gain_stack, gain_first, gain_second):
    positions = jnp.arange(SLOT, dtype=jnp.int32)
    weight = ((positions[None, :] < target_length[:, None]) & (target_keep > 0)).astype(jnp.float32)
    member = (language[:, None] == jnp.arange(NLANG, dtype=jnp.int32)[None, :]).astype(jnp.float32)
    counts = lax.optimization_barrier(jnp.sum(member * lax.optimization_barrier(jnp.sum(weight, axis=1, keepdims=True)), axis=0))
    inverse = 1.0 / (NLANG * jnp.maximum(counts, 1.0))
    scale = weight * lax.optimization_barrier(jnp.sum(member * inverse[None, :], axis=1, keepdims=True))

    def total_loss(attn_w, feed_w, table_w, gain_w):
        attn_b = low(attn_w)
        feed_b = low(feed_w)
        table_b = low(table_w)

        def per_sequence(carry, item):
            return (carry + sequence_loss(attn_b, feed_b, table_b, gain_w, item), None)
        total, _ = lax.scan(jax.checkpoint(per_sequence), jnp.zeros((), jnp.float32), (source_bytes, decoder_bytes, target_bytes, scale, source_length, target_length))
        return total
    loss, pull = jax.vjp(total_loss, attn_weights, to_matrix(feed_weights), table_weights, norm_gain_stack)
    attn_grad, feed_matrix_grad, table_grad, gain_grad = pull(jnp.ones((), jnp.float32))
    feed_grad = from_matrix(feed_matrix_grad)
    squares = jnp.sum(attn_grad * attn_grad) + jnp.sum(feed_grad * feed_grad) + jnp.sum(table_grad * table_grad) + jnp.sum(gain_grad * gain_grad)
    grad_norm = jnp.sqrt(squares)
    clip = CLIP_NORM / jnp.maximum(grad_norm, CLIP_NORM)
    count = step_count[0].astype(jnp.float32)
    attn_rate = jnp.array([MATRIX_RATE, MATRIX_RATE, MATRIX_RATE, (SLOT / (3.0 * INNER)) ** 0.5], jnp.float32)[None, :, None, None]
    table_rate = jnp.array([1.0, 1.5 * D ** (-0.5)], jnp.float32)[:, None, None]
    attn_new = adam(attn_weights, attn_first, attn_second, attn_grad, clip, count, attn_rate, DECAY_STEP)
    feed_new = adam(feed_weights, feed_first, feed_second, feed_grad, clip, count, MATRIX_RATE, DECAY_STEP)
    table_new = adam(table_weights, table_first, table_second, table_grad, clip, count, table_rate, DECAY_STEP)
    gain_new = adam(norm_gain_stack, gain_first, gain_second, gain_grad, clip, count, GAIN_RATE, 0.0)
    return (loss, grad_norm, attn_new[0], attn_new[1], attn_new[2], feed_new[0], feed_new[1], feed_new[2], table_new[0], table_new[1], table_new[2], gain_new[0], gain_new[1], gain_new[2])
```

```python
import functools

import jax
import jax.numpy as jnp
import numpy as np
from jax import lax
from jax.experimental import pallas as pl
from jax.experimental.pallas import tpu as pltpu
from jax.sharding import Mesh, PartitionSpec as P

D = 1472
HEADS = 6
HEAD_DIM = 64
NLANG = 4
INNER = 384
FF = 3584
LANES = 128
HALF = 768
WIDE = 2 * HALF

RMS_EPS = 1e-06
CLIP_NORM = 0.01
BETA_FIRST = 0.9
BETA_SECOND = 0.999
ADAM_EPS = 1e-08
MATRIX_RATE = 0.05
GAIN_RATE = 0.2
DECAY_STEP = 0.005
MASKED = -1000000000.0
PERIOD = 896
VMEM_LIMIT = 44 * 1024 * 1024
BF = jnp.bfloat16
F32 = jnp.float32


def dot_nn(a, b):
    return lax.dot_general(a, b, (((1,), (0,)), ((), ())), preferred_element_type=F32)


def dot_nt(a, b):
    return lax.dot_general(a, b, (((1,), (1,)), ((), ())), preferred_element_type=F32)


def dot_tn(a, b):
    return lax.dot_general(a, b, (((0,), (0,)), ((), ())), preferred_element_type=F32)


def flat_pieces(hid):
    found = []
    for t in range(PERIOD // LANES):
        at = LANES * t
        while at < LANES * (t + 1):
            j = at // hid
            end = min(LANES * (t + 1), (j + 1) * hid)
            found.append((t, at - LANES * t, j, at - j * hid, end - at))
            at = end
    return found


def unflatten_kernel(hid, groups, flat_ref, spread_ref, out_ref, acc_ref):
    chunks = PERIOD // LANES
    acc_ref[...] = jnp.zeros_like(acc_ref)
    for t in range(chunks):
        rows = flat_ref[0, pl.ds(t, groups, stride=chunks), :].astype(BF)
        for piece_t, lane, j, first, length in flat_pieces(hid):
            if piece_t == t:
                placed = dot_tn(rows, spread_ref[j])
                acc_ref[first : first + length, :] += placed[lane : lane + length, :]
    out_ref[0] = acc_ref[...].astype(BF)


def unflatten(flat, spread, hid, groups):
    count, flat_rows, _ = flat.shape
    lanes = spread.shape[2]
    return pl.pallas_call(
        functools.partial(unflatten_kernel, hid, groups),
        out_shape=jax.ShapeDtypeStruct((count, hid, lanes), BF),
        grid=(count,),
        in_specs=[
            pl.BlockSpec((1, flat_rows, LANES), lambda i: (i, 0, 0)),
            pl.BlockSpec(spread.shape, lambda i: (0, 0, 0)),
        ],
        out_specs=pl.BlockSpec((1, hid, lanes), lambda i: (i, 0, 0)),
        scratch_shapes=[pltpu.VMEM((hid, lanes), F32)],
        compiler_params=pltpu.CompilerParams(vmem_limit_bytes=VMEM_LIMIT),
        name="unflatten",
    )(flat, spread)


def flatten_kernel(hid, groups, grad_ref, spread_ref, out_ref):
    chunks = PERIOD // LANES
    high = grad_ref[0].astype(BF)
    low = (grad_ref[0] - high.astype(F32)).astype(BF)
    for t in range(chunks):
        total = jnp.zeros((groups, LANES), F32)
        for piece_t, lane, j, first, length in flat_pieces(hid):
            if piece_t == t:
                for part in (high, low):
                    rows = part[first : first + length, :]
                    parts = []
                    if lane > 0:
                        parts.append(jnp.zeros((lane, rows.shape[1]), BF))
                    parts.append(rows)
                    if lane + length < LANES:
                        parts.append(jnp.zeros((LANES - lane - length, rows.shape[1]), BF))
                    rows = jnp.concatenate(parts, 0) if len(parts) > 1 else rows
                    total = total + dot_nt(spread_ref[j], rows)
        out_ref[0, pl.ds(t, groups, stride=chunks), :] = total


def flatten(grads, spread, hid, groups):
    count, _, lanes = grads.shape
    flat_rows = groups * PERIOD // LANES
    return pl.pallas_call(
        functools.partial(flatten_kernel, hid, groups),
        out_shape=jax.ShapeDtypeStruct((count, flat_rows, LANES), F32),
        grid=(count,),
        in_specs=[
            pl.BlockSpec((1, hid, lanes), lambda i: (i, 0, 0)),
            pl.BlockSpec(spread.shape, lambda i: (0, 0, 0)),
        ],
        out_specs=pl.BlockSpec((1, flat_rows, LANES), lambda i: (i, 0, 0)),
        compiler_params=pltpu.CompilerParams(vmem_limit_bytes=VMEM_LIMIT),
        name="flatten",
    )(grads, spread)


def head_lanes(shape, h):
    lane = lax.broadcasted_iota(jnp.int32, shape, 1)
    return (lane < HEAD_DIM) if h == 0 else (lane >= HEAD_DIM)


def attend_kernel(causal, where_ref, q_ref, kv0_ref, kv1_ref, kv2_ref, out_ref, pos_ref):
    count = q_ref.shape[0]
    length = kv0_ref.shape[0]
    blocks = length // count
    limit = where_ref[3 * blocks]
    first = where_ref[3 * blocks + 1]
    for p, kv_ref in enumerate((kv0_ref, kv1_ref, kv2_ref)):
        for b in range(blocks):
            pos_ref[:, b * count : (b + 1) * count] = (
                lax.broadcasted_iota(jnp.int32, (8, count), 1) + where_ref[p * blocks + b]
            )
        pos = pos_ref[0:1, :]
        allowed = pos < limit
        if causal:
            query = first + lax.broadcasted_iota(jnp.int32, (count, length), 0)
            allowed = allowed & (pos <= query)
        queries = q_ref[:, p * LANES : (p + 1) * LANES]
        context = []
        for h in range(2):
            own = jnp.where(head_lanes(queries.shape, h), queries, jnp.zeros_like(queries))
            scores = dot_nt(own, kv_ref[:, :LANES]) * HEAD_DIM ** (-0.5)
            scores = jnp.where(allowed, scores, MASKED)
            raised = jnp.exp(scores - jnp.max(scores, axis=1, keepdims=True))
            probs = raised * (1.0 / jnp.sum(raised, axis=1, keepdims=True))
            context.append(dot_nn(probs.astype(BF), kv_ref[:, LANES:]))
        out_ref[:, p * LANES : (p + 1) * LANES] = jnp.where(
            head_lanes(context[0].shape, 0), context[0], context[1]
        ).astype(BF)


def attend(where, queries, kv, causal):
    count = queries.shape[0]
    length = kv[0].shape[0]
    vmem = pl.BlockSpec(memory_space=pltpu.VMEM)
    return pl.pallas_call(
        functools.partial(attend_kernel, causal),
        out_shape=jax.ShapeDtypeStruct((count, INNER), BF),
        in_specs=[pl.BlockSpec(memory_space=pltpu.SMEM)] + [vmem] * 4,
        out_specs=vmem,
        scratch_shapes=[pltpu.VMEM((8, length), jnp.int32)],
        compiler_params=pltpu.CompilerParams(vmem_limit_bytes=VMEM_LIMIT),
        cost_estimate=pl.CostEstimate(
            flops=4 * count * length * INNER * 2,
            transcendentals=HEADS * count * length,
            bytes_accessed=4 * length * INNER,
        ),
        name="attend",
    )(where, queries, *kv)


def attend_back_kernel(
    causal, where_ref, q_ref, g_ref, kv0_ref, kv1_ref, kv2_ref, dq_ref, d0_ref, d1_ref, d2_ref, pos_ref
):
    count = q_ref.shape[0]
    length = kv0_ref.shape[0]
    blocks = length // count
    limit = where_ref[3 * blocks]
    first = where_ref[3 * blocks + 1]
    scale = HEAD_DIM ** (-0.5)
    for p, (kv_ref, d_ref) in enumerate(((kv0_ref, d0_ref), (kv1_ref, d1_ref), (kv2_ref, d2_ref))):
        for b in range(blocks):
            pos_ref[b * count : (b + 1) * count, :] = (
                lax.broadcasted_iota(jnp.int32, (count, count), 0) + where_ref[p * blocks + b]
            )
        pos = pos_ref[...]
        allowed = pos < limit
        if causal:
            query = first + lax.broadcasted_iota(jnp.int32, (length, count), 1)
            allowed = allowed & (pos <= query)
        queries = q_ref[:, p * LANES : (p + 1) * LANES]
        grads = g_ref[:, p * LANES : (p + 1) * LANES]
        d_query, d_key, d_value = [], None, None
        for h in range(2):
            own_q = jnp.where(head_lanes(queries.shape, h), queries, jnp.zeros_like(queries))
            own_g = jnp.where(head_lanes(grads.shape, h), grads, jnp.zeros_like(grads))
            scores = dot_nt(kv_ref[:, :LANES], own_q) * scale
            scores = jnp.where(allowed, scores, MASKED)
            raised = jnp.exp(scores - jnp.max(scores, axis=0, keepdims=True))
            probs = raised * (1.0 / jnp.sum(raised, axis=0, keepdims=True))
            d_probs = dot_nt(kv_ref[:, LANES:], own_g)
            inner = jnp.sum(probs * d_probs, axis=0, keepdims=True)
            d_scores = (probs * (d_probs - inner)).astype(BF)
            d_query.append(dot_tn(d_scores, kv_ref[:, :LANES]) * scale)
            key_part = dot_nn(d_scores, own_q) * scale
            value_part = dot_nn(probs.astype(BF), own_g)
            d_key = key_part if h == 0 else d_key + key_part
            d_value = value_part if h == 0 else d_value + value_part
        dq_ref[:, p * LANES : (p + 1) * LANES] = jnp.where(
            head_lanes(d_query[0].shape, 0), d_query[0], d_query[1]
        ).astype(BF)
        d_ref[:, :LANES] = d_key.astype(BF)
        d_ref[:, LANES:] = d_value.astype(BF)


def attend_back(where, queries, grads, kv, causal):
    count = queries.shape[0]
    length = kv[0].shape[0]
    vmem = pl.BlockSpec(memory_space=pltpu.VMEM)
    part = jax.ShapeDtypeStruct((length, 2 * LANES), BF)
    out = pl.pallas_call(
        functools.partial(attend_back_kernel, causal),
        out_shape=(jax.ShapeDtypeStruct((count, INNER), BF), part, part, part),
        in_specs=[pl.BlockSpec(memory_space=pltpu.SMEM)] + [vmem] * 5,
        out_specs=(vmem,) * 4,
        scratch_shapes=[pltpu.VMEM((length, count), jnp.int32)],
        compiler_params=pltpu.CompilerParams(vmem_limit_bytes=VMEM_LIMIT),
        cost_estimate=pl.CostEstimate(
            flops=10 * count * length * INNER * 2,
            transcendentals=HEADS * count * length,
            bytes_accessed=8 * length * INNER,
        ),
        name="attend_back",
    )(where, queries, grads, *kv)
    return out[0], list(out[1:])


def rms_scale(stream):
    return lax.rsqrt(jnp.sum(stream * stream, axis=-1, keepdims=True) * (1.0 / D) + RMS_EPS)


def rms_reverse(stream, gain, scale, grad_out):
    weighted = grad_out * gain
    inner_mean = jnp.sum(weighted * stream, axis=-1, keepdims=True) * (1.0 / D)
    grad_in = scale * weighted - stream * (scale * scale * scale) * inner_mean
    grad_gain = jnp.sum(grad_out * stream * scale, axis=0)
    return (grad_in, grad_gain)


def gated_units(gate, upper):
    return jax.nn.gelu(gate, approximate=True) * upper


def adam(weight, first, second, grad, clip, count, rate, decay_step):
    clipped = grad * clip
    first_new = BETA_FIRST * first + (1.0 - BETA_FIRST) * clipped
    second_new = BETA_SECOND * second + (1.0 - BETA_SECOND) * clipped * clipped
    fixed_first = first_new / (1.0 - BETA_FIRST**count)
    fixed_second = second_new / (1.0 - BETA_SECOND**count)
    master = (
        weight - rate * (fixed_first / (jnp.sqrt(fixed_second) + ADAM_EPS)) - decay_step * weight
    )
    return (first_new, second_new, master)


class Links:
    def __init__(self, groups):
        self.groups = groups
        self.z_bits = [f"z{i}" for i in range(groups.bit_length() - 1)]
        self.near = self.z_bits[:-1] if len(self.z_bits) > 1 else []

    def swap(self, value, bit):
        if bit[0] == "z":
            step = 1 << int(bit[1:])
            return lax.ppermute(value, "z", [(i, i ^ step) for i in range(self.groups)])
        return lax.ppermute(value, bit, [(0, 1), (1, 0)])

    def swap_by_core(self, value, bits):
        pairs = []
        for c in range(2):
            for y in range(2):
                for x in range(2):
                    to = (y, x ^ 1) if bits[c] == "x" else (y ^ 1, x)
                    pairs.append((c * 4 + y * 2 + x, c * 4 + to[0] * 2 + to[1]))
        return lax.ppermute(value, ("c", "y", "x"), pairs)

    def ring(self, value, step):
        n = self.groups
        return lax.ppermute(value, "z", [(i, (i + step) % n) for i in range(n)])

    def plane_gather(self, own):
        first = self.swap_by_core(own, "xy")
        pair = jnp.concatenate([own, first], 0)
        second = self.swap_by_core(pair, "yx")
        mine = jnp.concatenate([pair, second], 0)
        return jnp.concatenate([mine, self.swap(mine, "c")], 0)

    def plane_scatter(self, parts):
        rows = parts.shape[0] // 8
        total = parts[: 4 * rows] + self.swap(parts[4 * rows :].astype(BF), "c").astype(F32)
        far = self.swap_by_core(total[2 * rows :].astype(BF), "yx").astype(F32)
        total = total[: 2 * rows] + far
        near = self.swap_by_core(total[rows:].astype(BF), "xy").astype(F32)
        return total[:rows] + near

    def orders(self):
        dims = ["x", "y"] + self.near
        return [[dims[(i + p) % len(dims)] for i in range(len(dims))] for p in range(3)]

    def sequence_gather(self, parts):
        out = []
        for part, order in zip(parts, self.orders()):
            for bit in order + ["c"]:
                part = jnp.concatenate([part, self.swap(part, bit)], 0)
            out.append(part)
        return out

    def sequence_scatter(self, parts):
        out = []
        for part, order in zip(parts, self.orders()):
            for bit in ["c"] + order[::-1]:
                rows = part.shape[0] // 2
                part = part[:rows].astype(F32) + self.swap(part[rows:].astype(BF), bit).astype(F32)
            out.append(part)
        return out

    def owner_scatter(self, grads, width):
        dims = self.z_bits[::-1] + ["y", "x"]
        count = grads.shape[0]
        far = [b for b in self.z_bits if b not in self.near]
        out = []
        for p, order in enumerate(self.orders()):
            part = grads[:, :, p * 256 : (p + 1) * 256]
            part = part.reshape([count] + [2] * len(dims) + [width, 256])
            left = list(dims)
            for bit in order + far:
                axis = 1 + left.index(bit)
                left.remove(bit)
                send = lax.index_in_dim(part, 1, axis, keepdims=False).astype(BF)
                keep = lax.index_in_dim(part, 0, axis, keepdims=False).astype(F32)
                part = keep + self.swap(send, bit).astype(F32)
            out.append(part)
        return jnp.concatenate(out, -1)

    def total(self, value, rows_high):
        for bit in ["c", "x", "y"] + self.z_bits:
            value = value + self.swap(value, bit)
        return lax.psum(value, "rh") if rows_high > 1 else value


def step(
    shape,
    source_bytes,
    decoder_bytes,
    target_bytes,
    target_keep,
    source_length,
    target_length,
    language,
    step_count,
    attn_weights,
    attn_first,
    attn_second,
    feed_weights,
    feed_first,
    feed_second,
    table_weights,
    table_first,
    table_second,
    norm_gain_stack,
    gain_first,
    gain_second,
):
    rows_high, groups = shape
    rows_n, cols_n = 2 * rows_high, 4 * groups
    links = Links(groups)
    core, zc, yc, xc = (lax.axis_index(a) for a in ("c", "z", "y", "x"))
    on_first = core == 0
    tokens = source_bytes.shape[1]
    chunk = attn_weights.shape[2]
    width = attn_weights.shape[3]
    everywhere = ("rh", "c", "z", "y", "x")

    def own_half(value):
        return jnp.where(on_first, value[..., :HALF], value[..., HALF:])

    def other_half(value):
        return jnp.where(on_first, value[..., HALF:], value[..., :HALF])

    def in_order(own, other, axis):
        return jnp.concatenate(
            [jnp.where(on_first, own, other), jnp.where(on_first, other, own)], axis
        )

    def widen(value):
        pad = [(0, 0)] * (value.ndim - 1) + [(0, HALF - value.shape[-1])]
        return jnp.pad(value, pad)

    def spread_features(value):
        split = value.reshape(value.shape[0], rows_high, 2, chunk).transpose(0, 2, 1, 3)
        return widen(split.reshape(value.shape[0], 2, D // 2)).reshape(value.shape[0], WIDE)

    def join_features(value):
        split = value.reshape(value.shape[0], 2, HALF)[:, :, : D // 2]
        split = split.reshape(value.shape[0], 2, rows_high, chunk).transpose(0, 2, 1, 3)
        return split.reshape(value.shape[0], D)

    half = groups // 2
    packed = jnp.concatenate(
        [source_bytes, decoder_bytes, target_bytes, target_keep]
        + [
            jnp.broadcast_to(v[:, None], (1, tokens))
            for v in (source_length, target_length, language, language)
        ],
        0,
    )
    pairs = []
    for c in range(2):
        for k in range(cols_n):
            block = (((k // 4) % half) * 4 + k % 4) * 2 + c
            pairs.append(((k // 4 // half) * cols_n + block, c * cols_n + k))
    packed = lax.ppermute(packed, ("c", "z", "y", "x"), pairs)
    block = (((zc % half) * 2 + yc) * 2 + xc) * 2 + core
    first_pos = block * tokens
    src_limit, tgt_limit, tongue = packed[4, 0], packed[5, 0], packed[6, 0]
    positions = first_pos + jnp.arange(tokens, dtype=jnp.int32)
    weight = ((positions < tgt_limit) & (packed[3] > 0)).astype(F32)
    member = (tongue == jnp.arange(LANES, dtype=jnp.int32)).astype(F32)
    counts = links.total(jnp.broadcast_to((member * jnp.sum(weight))[None], (8, LANES)), rows_high)
    inverse = 1.0 / (NLANG * jnp.maximum(counts[0], 1.0))
    token_scale = weight * jnp.sum(member * inverse)

    bit_value = {"c": 1, "x": 2, "y": 4}
    for i, bit in enumerate(links.near):
        bit_value[bit] = 8 << i
    masks = []
    for order in links.orders():
        mask = [0]
        for bit in order + ["c"]:
            mask = mask + [m ^ bit_value[bit] for m in mask]
        masks.append(mask)
    firsts = (jnp.array(np.array(masks).reshape(-1), jnp.int32) ^ block) * tokens

    def places(limit):
        return jnp.concatenate([firsts, jnp.stack([limit, first_pos]).astype(jnp.int32)])

    src_places, tgt_places = places(src_limit), places(tgt_limit)

    attn_t = attn_weights.transpose(0, 1, 3, 2)
    table_t = table_weights.transpose(0, 2, 1)

    def gather_tiles(tiles):
        tiles = tiles.astype(BF)
        if rows_high == 1:
            tiles = widen(tiles)
        full = lax.all_gather(tiles[:, None], everywhere, axis=1, tiled=True)
        if rows_high == 1:
            return full.reshape(tiles.shape[0], 2, INNER, HALF)
        full = full.reshape(tiles.shape[0], rows_high, 2, INNER, chunk).transpose(0, 2, 3, 1, 4)
        return widen(full.reshape(tiles.shape[0], 2, INNER, D // 2))

    early = gather_tiles(jnp.concatenate([attn_t[0], table_t[:1]], 0))
    late = gather_tiles(jnp.concatenate([attn_t[1], attn_t[2], table_t[1:]], 0))
    weights = [early[:4], late[:4], late[4:8]]
    embed_w, head_w = early[4], late[8]

    def project(value, matrix):
        return dot_nt(value[:, :HALF], matrix[0]) + dot_nt(value[:, HALF:], matrix[1])

    def unproject(value, matrix):
        return jnp.concatenate([dot_nn(value, matrix[0]), dot_nn(value, matrix[1])], 1)

    hid = FF // cols_n
    hid_half = hid // 2
    period_rows = PERIOD // hid
    period_groups = chunk // period_rows
    lanes_own = HALF if rows_high == 1 else chunk
    shape3 = (period_rows, period_groups, lanes_own)
    spread = (
        lax.broadcasted_iota(jnp.int32, shape3, 2)
        == lax.broadcasted_iota(jnp.int32, shape3, 1) * period_rows
        + lax.broadcasted_iota(jnp.int32, shape3, 0)
    ).astype(BF)
    flat_shape = (6, chunk * hid // LANES, LANES)
    feed_t = unflatten(feed_weights.reshape(flat_shape), spread, hid, period_groups)
    if rows_high > 1:
        feed_t = lax.all_gather(feed_t[None], "rh", axis=0, tiled=True)
        feed_t = widen(feed_t.transpose(1, 2, 0, 3).reshape(6, hid, D // 2))

    def ring_gather(mine):
        keep = jnp.where(on_first, mine[:, :hid_half], mine[:, hid_half:])
        send = jnp.where(on_first, mine[:, hid_half:], mine[:, :hid_half])
        value = in_order(keep, links.swap(send, "c"), 2)
        held = [value]
        for _ in range(groups - 1):
            held.append(links.ring(held[-1], 1))
        return [jnp.concatenate([h[m] for h in held], 0) for m in range(3)]

    def ring_scatter(grads):
        grads = [g.reshape(groups, hid_half, WIDE) for g in grads]

        def at(s):
            return jnp.stack([g[s] for g in grads])

        value = at(groups - 1)
        for s in range(groups - 2, -1, -1):
            value = at(s).astype(F32) + links.ring(value.astype(BF), -1).astype(F32)
        keep, send = own_half(value), other_half(value)
        full = in_order(keep, links.swap(send.astype(BF), "c").astype(F32), 1)
        if rows_high > 1:
            full = full[:, :, : D // 2].reshape(3, hid, rows_high, chunk)
            full = lax.psum_scatter(full, "rh", scatter_dimension=2, tiled=True)
            full = full.reshape(3, hid, chunk)
        return full

    feed_b = [ring_gather(feed_t[:3]), ring_gather(feed_t[3:])]
    gains = spread_features(norm_gain_stack)

    def norm(stream, index):
        scale = rms_scale(stream)
        return (stream * scale * gains[index]).astype(BF), scale

    def key_value_parts(normed, matrices):
        keys = project(normed, matrices[1]).astype(BF)
        values = project(normed, matrices[2]).astype(BF)
        return [
            jnp.concatenate(
                [keys[:, p * LANES : (p + 1) * LANES], values[:, p * LANES : (p + 1) * LANES]], 1
            )
            for p in range(3)
        ]

    def attention(normed_q, normed_kv, matrices, where, causal):
        queries = project(normed_q, matrices[0]).astype(BF)
        kv = links.sequence_gather(key_value_parts(normed_kv, matrices))
        context = attend(where, queries, kv, causal)
        return unproject(context, matrices[3]), (queries, kv, context)

    def feed(normed, matrices):
        everyone = links.plane_gather(normed)
        gate = dot_nt(everyone, matrices[0])
        upper = dot_nt(everyone, matrices[1])
        hidden = gated_units(gate, upper).astype(BF)
        return links.plane_scatter(dot_nn(hidden, matrices[2])), (everyone, gate, upper, hidden)

    vocab_ids = jnp.arange(INNER, dtype=jnp.int32)
    src_hot = (packed[0][:, None] == vocab_ids).astype(BF)
    dec_hot = (packed[1][:, None] == vocab_ids).astype(BF)
    enc_zero = unproject(src_hot, embed_w)
    dec_zero = unproject(dec_hot, embed_w)
    n_zero, s_zero = norm(enc_zero, 0)
    branch, kept_enc = attention(n_zero, n_zero, weights[0], src_places, False)
    enc_one = enc_zero + branch
    n_one, s_one = norm(enc_one, 1)
    branch, kept_enc_feed = feed(n_one, feed_b[0])
    enc_two = enc_one + branch
    memory, s_two = norm(enc_two, 2)
    n_three, s_three = norm(dec_zero, 3)
    branch, kept_dec = attention(n_three, n_three, weights[1], tgt_places, True)
    dec_one = dec_zero + branch
    n_four, s_four = norm(dec_one, 4)
    branch, kept_cross = attention(n_four, memory, weights[2], src_places, False)
    dec_two = dec_one + branch
    n_five, s_five = norm(dec_two, 5)
    branch, kept_dec_feed = feed(n_five, feed_b[1])
    dec_three = dec_two + branch
    final, s_six = norm(dec_three, 6)

    logits = project(final, head_w)
    lse = jax.nn.logsumexp(logits, axis=-1)
    target_hot = (packed[2][:, None] == vocab_ids).astype(F32)
    picked = jnp.sum(logits * target_hot, axis=-1)
    loss_local = jnp.sum((lse - picked) * token_scale)
    grad_logits = ((jnp.exp(logits - lse[:, None]) - target_hot) * token_scale[:, None]).astype(BF)

    own_index = zc * 4 + yc * 2 + xc
    columns = jnp.arange(INNER, dtype=jnp.int32)
    moved = ((columns // width) ^ own_index) * width + columns % width
    shuffle = (columns[:, None] == moved[None, :]).astype(BF)

    def relative(value):
        return dot_nn(value, shuffle).astype(BF)

    def weight_grads(pairs):
        out = []
        for cols, feats in pairs:
            count = cols.shape[1] // INNER
            send = dot_tn(cols, other_half(feats)).astype(BF).reshape(count, INNER, HALF)
            keep = dot_tn(cols, own_half(feats)).reshape(count, INNER, HALF)
            out.append(keep + links.swap(send, "c").astype(F32))
        return jnp.concatenate(out, 0)

    def feed_back(kept, matrices, grad):
        everyone, gate, upper, hidden = kept
        grad_all = links.plane_gather(grad.astype(BF))
        _, pull = jax.vjp(gated_units, gate, upper)
        grad_gate, grad_upper = pull(dot_nt(grad_all, matrices[2]))
        gate_b, upper_b = grad_gate.astype(BF), grad_upper.astype(BF)
        grad_normed = links.plane_scatter(
            dot_nn(gate_b, matrices[0]) + dot_nn(upper_b, matrices[1])
        )
        grads = [
            dot_tn(gate_b, everyone).astype(BF),
            dot_tn(upper_b, everyone).astype(BF),
            dot_tn(hidden, grad_all).astype(BF),
        ]
        return grad_normed, grads

    def attention_back(kept, normed_q, normed_kv, matrices, where, causal, grad):
        queries, kv, context = kept
        grad_b = grad.astype(BF)
        grad_context = project(grad_b, matrices[3]).astype(BF)
        d_query, d_parts = attend_back(where, queries, grad_context, kv, causal)
        d_parts = [p.astype(BF) for p in links.sequence_scatter(d_parts)]
        d_key = jnp.concatenate([p[:, :LANES] for p in d_parts], 1)
        d_value = jnp.concatenate([p[:, LANES:] for p in d_parts], 1)
        d_normed_q = unproject(d_query, matrices[0])
        d_normed_kv = unproject(d_key, matrices[1]) + unproject(d_value, matrices[2])
        cols = [relative(v) for v in (d_query, d_key, d_value, context)]
        if normed_q is normed_kv:
            grads = weight_grads(
                [(jnp.concatenate(cols[:3], 1), normed_q), (cols[3], grad_b)]
            )
        else:
            grads = weight_grads(
                [(cols[0], normed_q), (jnp.concatenate(cols[1:3], 1), normed_kv), (cols[3], grad_b)]
            )
        return d_normed_q, d_normed_kv, grads

    head_grad = weight_grads([(relative(grad_logits), final)])
    grad_final = unproject(grad_logits, head_w)
    grad_dec, gain_six = rms_reverse(dec_three, gains[6], s_six, grad_final)
    grad_normed, feed_dec_grad = feed_back(kept_dec_feed, feed_b[1], grad_dec)
    part, gain_five = rms_reverse(dec_two, gains[5], s_five, grad_normed)
    grad_dec = grad_dec + part
    d_q, grad_memory, cross_grad = attention_back(
        kept_cross, n_four, memory, weights[2], src_places, False, grad_dec
    )
    part, gain_four = rms_reverse(dec_one, gains[4], s_four, d_q)
    grad_dec = grad_dec + part
    d_q, d_kv, dec_grad = attention_back(
        kept_dec, n_three, n_three, weights[1], tgt_places, True, grad_dec
    )
    part, gain_three = rms_reverse(dec_zero, gains[3], s_three, d_q + d_kv)
    grad_dec = grad_dec + part
    grad_enc, gain_two = rms_reverse(enc_two, gains[2], s_two, grad_memory)
    grad_normed, feed_enc_grad = feed_back(kept_enc_feed, feed_b[0], grad_enc)
    part, gain_one = rms_reverse(enc_one, gains[1], s_one, grad_normed)
    grad_enc = grad_enc + part
    d_q, d_kv, enc_grad = attention_back(
        kept_enc, n_zero, n_zero, weights[0], src_places, False, grad_enc
    )
    part, gain_zero = rms_reverse(enc_zero, gains[0], s_zero, d_q + d_kv)
    grad_enc = grad_enc + part
    hot = jnp.concatenate([relative(src_hot), relative(dec_hot)], 0)
    streams = jnp.concatenate([grad_enc, grad_dec], 0)
    stream_high = streams.astype(BF)
    stream_low = (streams - stream_high.astype(F32)).astype(BF)
    embed_grad = weight_grads(
        [(jnp.concatenate([hot, hot], 0), jnp.concatenate([stream_high, stream_low], 0))]
    )

    late_red = links.owner_scatter(jnp.concatenate([dec_grad, cross_grad, head_grad], 0), width)
    early_red = links.owner_scatter(jnp.concatenate([enc_grad, embed_grad], 0), width)

    def own_chunk(value):
        value = value[:, :, : D // 2]
        if rows_high > 1:
            value = value.reshape(value.shape[0], width, rows_high, chunk)
            value = lax.psum_scatter(value, "rh", scatter_dimension=2, tiled=True)
            value = value.reshape(value.shape[0], width, chunk)
        return value

    late_red, early_red = own_chunk(late_red), own_chunk(early_red)
    attn_red = jnp.stack([early_red[:4], late_red[:4], late_red[4:8]])
    table_red = jnp.stack([early_red[4], late_red[8]])
    feed_red = [
        flatten(ring_scatter(g), spread, hid, period_groups) for g in (feed_enc_grad, feed_dec_grad)
    ]
    feed_red = jnp.stack(feed_red)
    square_local = (
        jnp.sum(attn_red * attn_red) + jnp.sum(table_red * table_red) + jnp.sum(feed_red * feed_red)
    )
    lane = jnp.arange(WIDE)
    extra = jnp.where(lane == 0, square_local, 0.0) + jnp.where(lane == 1, loss_local, 0.0)
    gain_local = jnp.stack(
        [gain_zero, gain_one, gain_two, gain_three, gain_four, gain_five, gain_six, extra]
    )
    everything = links.total(gain_local, rows_high)
    loss = everything[7, 1]
    gain_red = join_features(everything[:7])
    grad_norm = jnp.sqrt(everything[7, 0] + jnp.sum(gain_red * gain_red))
    clip = CLIP_NORM / jnp.maximum(grad_norm, CLIP_NORM)
    count = step_count[0].astype(F32)
    slot_total = tokens * cols_n
    attn_rate = jnp.array(
        [MATRIX_RATE, MATRIX_RATE, MATRIX_RATE, (slot_total / (3.0 * INNER)) ** 0.5], F32
    )[None, :, None, None]
    table_rate = jnp.array([1.0, 1.5 * D ** (-0.5)], F32)[:, None, None]

    def attn_turn(value):
        return value.transpose(0, 1, 3, 2)

    def table_turn(value):
        return value.transpose(0, 2, 1)

    attn_new = adam(
        attn_t, attn_turn(attn_first), attn_turn(attn_second), attn_red, clip, count, attn_rate, DECAY_STEP
    )
    feed_shape = (2, 3) + flat_shape[1:]
    feed_new = adam(
        feed_weights.reshape(feed_shape),
        feed_first.reshape(feed_shape),
        feed_second.reshape(feed_shape),
        feed_red,
        clip,
        count,
        MATRIX_RATE,
        DECAY_STEP,
    )
    table_new = adam(
        table_t, table_turn(table_first), table_turn(table_second), table_red, clip, count, table_rate, DECAY_STEP
    )
    gain_new = adam(norm_gain_stack, gain_first, gain_second, gain_red, clip, count, GAIN_RATE, 0.0)
    return (
        (loss, grad_norm)
        + tuple(attn_turn(v) for v in attn_new)
        + tuple(v.reshape(feed_weights.shape) for v in feed_new)
        + tuple(table_turn(v) for v in table_new)
        + tuple(gain_new)
    )


def solution(mesh):
    rows_high = mesh.shape["row"] // 2
    groups = mesh.shape["col"] // 4
    split = Mesh(mesh.devices.reshape(rows_high, 2, groups, 2, 2), ("rh", "c", "z", "y", "x"))
    row, col = ("rh", "c"), ("z", "y", "x")
    attn = P(None, None, row, col)
    feed = P(None, None, col, row)
    table = P(None, row, col)
    ids = P(row, col)
    in_specs = (ids,) * 4 + (P(row),) * 3 + (P(),) + (attn,) * 3 + (feed,) * 3 + (table,) * 3 + (P(),) * 3
    out_specs = (P(), P()) + (attn,) * 3 + (feed,) * 3 + (table,) * 3 + (P(),) * 3
    return jax.shard_map(
        functools.partial(step, (rows_high, groups)),
        mesh=split,
        in_specs=in_specs,
        out_specs=out_specs,
        check_vma=False,
    )
```

```python
import functools

import jax
import jax.numpy as jnp
import numpy as np
from jax import lax
from jax.experimental import pallas as pl
from jax.experimental.pallas import tpu as pltpu
from jax.sharding import Mesh, PartitionSpec as P

D = 1472
HEADS = 6
HEAD_DIM = 64
NLANG = 4
INNER = 384
FF = 3584
LANES = 128
HALF = 768
WIDE = 2 * HALF

RMS_EPS = 1e-06
CLIP_NORM = 0.01
BETA_FIRST = 0.9
BETA_SECOND = 0.999
ADAM_EPS = 1e-08
MATRIX_RATE = 0.05
GAIN_RATE = 0.2
DECAY_STEP = 0.005
MASKED = -1000000000.0
PERIOD = 896
MIB = 1024 * 1024
BF = jnp.bfloat16
F32 = jnp.float32


def dot_nn(a, b):
    return lax.dot_general(a, b, (((1,), (0,)), ((), ())), preferred_element_type=F32)


def dot_nt(a, b):
    return lax.dot_general(a, b, (((1,), (1,)), ((), ())), preferred_element_type=F32)


def dot_tn(a, b):
    return lax.dot_general(a, b, (((0,), (0,)), ((), ())), preferred_element_type=F32)


def flat_pieces(hid):
    found = []
    for t in range(PERIOD // LANES):
        at = LANES * t
        while at < LANES * (t + 1):
            j = at // hid
            end = min(LANES * (t + 1), (j + 1) * hid)
            found.append((t, at - LANES * t, j, at - j * hid, end - at))
            at = end
    return found


def unflatten_kernel(hid, groups, flat_ref, spread_ref, out_ref, acc_ref):
    chunks = PERIOD // LANES
    acc_ref[...] = jnp.zeros_like(acc_ref)
    for t in range(chunks):
        rows = flat_ref[0, pl.ds(t, groups, stride=chunks), :].astype(BF)
        for piece_t, lane, j, first, length in flat_pieces(hid):
            if piece_t == t:
                placed = dot_tn(rows, spread_ref[j])
                acc_ref[first : first + length, :] += placed[lane : lane + length, :]
    out_ref[0] = acc_ref[...].astype(BF)


def unflatten(flat, spread, hid, groups):
    count, flat_rows, _ = flat.shape
    lanes = spread.shape[2]
    return pl.pallas_call(
        functools.partial(unflatten_kernel, hid, groups),
        out_shape=jax.ShapeDtypeStruct((count, hid, lanes), BF),
        grid=(count,),
        in_specs=[
            pl.BlockSpec((1, flat_rows, LANES), lambda i: (i, 0, 0)),
            pl.BlockSpec(spread.shape, lambda i: (0, 0, 0)),
        ],
        out_specs=pl.BlockSpec((1, hid, lanes), lambda i: (i, 0, 0)),
        scratch_shapes=[pltpu.VMEM((hid, lanes), F32)],
        compiler_params=pltpu.CompilerParams(vmem_limit_bytes=10 * MIB),
        name="unflatten",
    )(flat, spread)


def flatten_kernel(hid, groups, grad_ref, spread_ref, out_ref):
    chunks = PERIOD // LANES
    high = grad_ref[0].astype(BF)
    low = (grad_ref[0] - high.astype(F32)).astype(BF)
    for t in range(chunks):
        total = jnp.zeros((groups, LANES), F32)
        for piece_t, lane, j, first, length in flat_pieces(hid):
            if piece_t == t:
                for part in (high, low):
                    rows = part[first : first + length, :]
                    parts = []
                    if lane > 0:
                        parts.append(jnp.zeros((lane, rows.shape[1]), BF))
                    parts.append(rows)
                    if lane + length < LANES:
                        parts.append(jnp.zeros((LANES - lane - length, rows.shape[1]), BF))
                    rows = jnp.concatenate(parts, 0) if len(parts) > 1 else rows
                    total = total + dot_nt(spread_ref[j], rows)
        out_ref[0, pl.ds(t, groups, stride=chunks), :] = total


def flatten(grads, spread, hid, groups):
    count, _, lanes = grads.shape
    flat_rows = groups * PERIOD // LANES
    return pl.pallas_call(
        functools.partial(flatten_kernel, hid, groups),
        out_shape=jax.ShapeDtypeStruct((count, flat_rows, LANES), F32),
        grid=(count,),
        in_specs=[
            pl.BlockSpec((1, hid, lanes), lambda i: (i, 0, 0)),
            pl.BlockSpec(spread.shape, lambda i: (0, 0, 0)),
        ],
        out_specs=pl.BlockSpec((1, flat_rows, LANES), lambda i: (i, 0, 0)),
        compiler_params=pltpu.CompilerParams(vmem_limit_bytes=10 * MIB),
        name="flatten",
    )(grads, spread)


def finish_kernel(
    slot_rate, scal_ref, all_ref, enc_ref, dec_ref, early_ref, own_ref, cross_ref, gain_ref,
    fw_ref, fm_ref, fv_ref, aw_ref, am_ref, av_ref, tw_ref, tm_ref, tv_ref, gw_ref, gm_ref, gv_ref,
    fm_out, fv_out, fw_out, am_out, av_out, aw_out, tm_out, tv_out, tw_out, gm_out, gv_out, gw_out,
):
    at = pl.program_id(0)
    gains = all_ref[0:7, :]
    square = jnp.sum(jnp.sum(gains * gains, axis=1, keepdims=True), axis=0, keepdims=True)
    norm = jnp.sqrt(all_ref[7:8, 0:1] + square)
    clip = CLIP_NORM / jnp.maximum(norm, CLIP_NORM)
    scales = (clip, scal_ref[0], scal_ref[1])

    def feed(grad_ref):
        fm_out[0], fv_out[0], fw_out[0] = adam_rule(
            fw_ref[0], fm_ref[0], fv_ref[0], grad_ref[0], *scales, MATRIX_RATE, DECAY_STEP
        )

    @pl.when(at < 3)
    def _():
        feed(enc_ref)

    @pl.when(at >= 3)
    def _():
        feed(dec_ref)

    chunk = aw_ref.shape[2]
    grads = [ref.at[i] for ref in (early_ref, own_ref, cross_ref) for i in range(4)]
    for i, grad in enumerate(grads):

        @pl.when(at == i // 2)
        def _(i=i, grad=grad):
            rate = slot_rate if i % 4 == 3 else MATRIX_RATE
            k = i % 2
            am_out[k], av_out[k], aw_out[k] = adam_rule(
                aw_ref[k], am_ref[k], av_ref[k], grad[:, :chunk], *scales, rate, DECAY_STEP
            )

    @pl.when(at == 5)
    def _():
        for i, (grad, rate) in enumerate(((early_ref.at[4], 1.0), (cross_ref.at[4], 1.5 * D ** (-0.5)))):
            tm_out[i], tv_out[i], tw_out[i] = adam_rule(
                tw_ref[i], tm_ref[i], tv_ref[i], grad[:, :chunk], *scales, rate, DECAY_STEP
            )
        gm_out[...], gv_out[...], gw_out[...] = adam_rule(
            gw_ref[...], gm_ref[...], gv_ref[...], gain_ref[...], *scales, GAIN_RATE, 0.0
        )


def finish(slot_rate, scalars, everything, feed_grads, rest_grads, feed, attn, table, gain):
    block = (1,) + feed[0].shape[1:]
    flat = pl.BlockSpec(block, lambda i: (i, 0, 0))

    def whole(value):
        return pl.BlockSpec(value.shape, lambda i: (0,) * value.ndim)

    def like(value):
        return jax.ShapeDtypeStruct(value.shape, F32)

    rest = table + gain
    pair = pl.BlockSpec((2,) + attn[0].shape[1:], lambda i: (i, 0, 0))
    return pl.pallas_call(
        functools.partial(finish_kernel, slot_rate),
        out_shape=[like(v) for v in feed + attn + rest],
        grid=(6,),
        in_specs=[pl.BlockSpec(memory_space=pltpu.SMEM), whole(everything)]
        + [
            pl.BlockSpec(block, lambda i: (jnp.minimum(i, 2), 0, 0)),
            pl.BlockSpec(block, lambda i: (jnp.maximum(i - 3, 0), 0, 0)),
        ]
        + [whole(v) for v in rest_grads]
        + [flat] * 3
        + [pair] * 3
        + [whole(v) for v in rest],
        out_specs=[flat] * 3 + [pair] * 3 + [whole(v) for v in rest],
        compiler_params=pltpu.CompilerParams(vmem_limit_bytes=56 * MIB),
        name="finish",
    )(scalars, everything, *feed_grads, *rest_grads, *feed, *attn, *rest)


def head_lanes(shape, h):
    lane = lax.broadcasted_iota(jnp.int32, shape, 1)
    return (lane < HEAD_DIM) if h == 0 else (lane >= HEAD_DIM)


def attend_kernel(causal, where_ref, q_ref, kv_ref, out_ref, pos_ref):
    count = q_ref.shape[0]
    length = kv_ref.shape[0]
    blocks = length // count
    limit = where_ref[blocks]
    first = where_ref[blocks + 1]
    for b in range(blocks):
        pos_ref[:, b * count : (b + 1) * count] = (
            lax.broadcasted_iota(jnp.int32, (8, count), 1) + where_ref[b]
        )
    pos = pos_ref[0:1, :]
    last = jnp.full((count, 1), limit - 1, jnp.int32)
    if causal:
        last = jnp.minimum(last, first + lax.broadcasted_iota(jnp.int32, (count, 1), 0))
    allowed = pos <= last
    for p in range(3):
        lanes = slice(p * LANES, (p + 1) * LANES)
        values = slice(INNER + p * LANES, INNER + (p + 1) * LANES)
        queries = q_ref[:, lanes] * HEAD_DIM ** (-0.5)
        context = []
        for h in range(2):
            own = jnp.where(head_lanes(queries.shape, h), queries, jnp.zeros_like(queries))
            scores = dot_nt(own, kv_ref[:, lanes])
            scores = jnp.where(allowed, scores, MASKED)
            raised = jnp.exp(scores - jnp.max(scores, axis=1, keepdims=True))
            probs = raised * (1.0 / jnp.sum(raised, axis=1, keepdims=True))
            context.append(dot_nn(probs.astype(BF), kv_ref[:, values]))
        out_ref[:, lanes] = jnp.where(
            head_lanes(context[0].shape, 0), context[0], context[1]
        ).astype(BF)


def attend(where, queries, kv, causal):
    count = queries.shape[0]
    length = kv.shape[0]
    vmem = pl.BlockSpec(memory_space=pltpu.VMEM)
    return pl.pallas_call(
        functools.partial(attend_kernel, causal),
        out_shape=jax.ShapeDtypeStruct((count, INNER), BF),
        in_specs=[pl.BlockSpec(memory_space=pltpu.SMEM)] + [vmem] * 2,
        out_specs=vmem,
        scratch_shapes=[pltpu.VMEM((8, length), jnp.int32)],
        compiler_params=pltpu.CompilerParams(vmem_limit_bytes=8 * MIB + 4096 * length),
        cost_estimate=pl.CostEstimate(
            flops=4 * count * length * INNER * 2,
            transcendentals=HEADS * count * length,
            bytes_accessed=4 * length * INNER,
        ),
        name="attend",
    )(where, queries, kv)


def attend_back_kernel(causal, where_ref, q_ref, g_ref, kv_ref, dq_ref, dkv_ref, pos_ref):
    count = q_ref.shape[0]
    length = kv_ref.shape[0]
    blocks = length // count
    limit = where_ref[blocks]
    first = where_ref[blocks + 1]
    scale = HEAD_DIM ** (-0.5)
    last = jnp.full((1, count), limit - 1, jnp.int32)
    if causal:
        last = jnp.minimum(last, first + lax.broadcasted_iota(jnp.int32, (1, count), 1))
    for b in range(blocks):
        pos_ref[b * count : (b + 1) * count, :] = (
            lax.broadcasted_iota(jnp.int32, (count, count), 0) + where_ref[b]
        )
    for p in range(3):
        lanes = slice(p * LANES, (p + 1) * LANES)
        values = slice(INNER + p * LANES, INNER + (p + 1) * LANES)
        allowed = pos_ref[...] <= last
        queries = q_ref[:, lanes] * scale
        grads = g_ref[:, lanes]
        d_query, d_key, d_value = [], None, None
        for h in range(2):
            own_q = jnp.where(head_lanes(queries.shape, h), queries, jnp.zeros_like(queries))
            own_g = jnp.where(head_lanes(grads.shape, h), grads, jnp.zeros_like(grads))
            scores = dot_nt(kv_ref[:, lanes], own_q)
            scores = jnp.where(allowed, scores, MASKED)
            raised = jnp.exp(scores - jnp.max(scores, axis=0, keepdims=True))
            probs = raised * (1.0 / jnp.sum(raised, axis=0, keepdims=True))
            d_probs = dot_nt(kv_ref[:, values], own_g)
            inner = jnp.sum(probs * d_probs, axis=0, keepdims=True)
            d_scores = (probs * (d_probs - inner)).astype(BF)
            d_query.append(dot_tn(d_scores, kv_ref[:, lanes]) * scale)
            key_part = dot_nn(d_scores, own_q)
            value_part = dot_nn(probs.astype(BF), own_g)
            d_key = key_part if h == 0 else d_key + key_part
            d_value = value_part if h == 0 else d_value + value_part
        dq_ref[:, lanes] = jnp.where(
            head_lanes(d_query[0].shape, 0), d_query[0], d_query[1]
        ).astype(BF)
        dkv_ref[:, lanes] = d_key.astype(BF)
        dkv_ref[:, values] = d_value.astype(BF)


def attend_back(where, queries, grads, kv, causal):
    count = queries.shape[0]
    length = kv.shape[0]
    vmem = pl.BlockSpec(memory_space=pltpu.VMEM)
    return pl.pallas_call(
        functools.partial(attend_back_kernel, causal),
        out_shape=(
            jax.ShapeDtypeStruct((count, INNER), BF),
            jax.ShapeDtypeStruct((length, 2 * INNER), BF),
        ),
        in_specs=[pl.BlockSpec(memory_space=pltpu.SMEM)] + [vmem] * 3,
        out_specs=(vmem,) * 2,
        scratch_shapes=[pltpu.VMEM((length, count), jnp.int32)],
        compiler_params=pltpu.CompilerParams(vmem_limit_bytes=8 * MIB + 8192 * length),
        cost_estimate=pl.CostEstimate(
            flops=10 * count * length * INNER * 2,
            transcendentals=HEADS * count * length,
            bytes_accessed=8 * length * INNER,
        ),
        name="attend_back",
    )(where, queries, grads, kv)


def rms_scale(stream):
    return lax.rsqrt(jnp.sum(stream * stream, axis=-1, keepdims=True) * (1.0 / D) + RMS_EPS)


def rms_reverse(stream, gain, scale, grad_out):
    weighted = grad_out * gain
    inner_mean = jnp.sum(weighted * stream, axis=-1, keepdims=True) * (1.0 / D)
    grad_in = scale * weighted - stream * (scale * scale * scale) * inner_mean
    grad_gain = jnp.sum(grad_out * stream * scale, axis=0)
    return (grad_in, grad_gain)


def gated_units(gate, upper):
    return jax.nn.gelu(gate, approximate=True) * upper


def adam_rule(weight, first, second, grad, clip, first_scale, second_scale, rate, decay_step):
    clipped = grad * clip
    first_new = BETA_FIRST * first + (1.0 - BETA_FIRST) * clipped
    second_new = BETA_SECOND * second + (1.0 - BETA_SECOND) * clipped * clipped
    ratio = first_new * first_scale / (jnp.sqrt(second_new * second_scale) + ADAM_EPS)
    return (first_new, second_new, weight - rate * ratio - decay_step * weight)


def anchor(value, *events):
    return lax.optimization_barrier((value,) + events)[0] if events else value


class Links:
    def __init__(self, groups):
        self.groups = groups
        self.z_bits = [f"z{i}" for i in range(groups.bit_length() - 1)]
        self.near = self.z_bits[:-1] if len(self.z_bits) > 1 else []
        self.cargo = []

    def load(self, *trips):
        self.cargo += [(trip, next(trip)) for trip in trips]

    def ship(self):
        trip, (value, step) = self.cargo.pop(0)
        return trip, self.ring(value, step)

    def land(self, trip, came):
        try:
            self.cargo.insert(min(1, len(self.cargo)), (trip, trip.send(came)))
        except StopIteration:
            pass

    def ride(self, value, count=1):
        sent = [self.ship() for _ in range(min(count, len(self.cargo)))]
        if sent:
            came = lax.optimization_barrier((value,) + tuple(c for _, c in sent))
            value = came[0]
            for (trip, _), c in zip(sent, came[1:]):
                self.land(trip, c)
        return value

    def unload(self):
        while self.cargo:
            self.land(*self.ship())

    def swap(self, value, bit):
        if bit[0] == "z":
            step = 1 << int(bit[1:])
            return lax.ppermute(value, "z", [(i, i ^ step) for i in range(self.groups)])
        return lax.ppermute(value, bit, [(0, 1), (1, 0)])

    def swap_by_core(self, value, bits):
        chips = 4 * self.groups
        masks = {"x": 1, "y": 2}
        for i, bit in enumerate(self.z_bits):
            masks[bit] = 4 << i
        pairs = [(c * chips + k, c * chips + (k ^ masks[bits[c]])) for c in range(2) for k in range(chips)]
        return lax.ppermute(value, ("c", "z", "y", "x"), pairs)

    def ring(self, value, step):
        n = self.groups
        return lax.ppermute(value, "z", [(i, (i + step) % n) for i in range(n)])

    def plane_gather(self, own, rides=(0, 0)):
        first = self.ride(self.swap_by_core(own, "xy"), rides[0])
        pair = jnp.concatenate([own, first], 0)
        second = self.ride(self.swap_by_core(pair, "yx"), rides[1])
        mine = jnp.concatenate([pair, second], 0)
        return jnp.concatenate([mine, self.swap(mine, "c")], 0)

    def plane_scatter(self, part_of, rides=(0, 0)):
        total = self.swap(part_of(4, 8).astype(BF), "c").astype(F32) + part_of(0, 4)
        rows = total.shape[0] // 4
        far = self.ride(self.swap_by_core(total[2 * rows :].astype(BF), "yx"), rides[0]).astype(F32)
        near = (total[rows : 2 * rows] + far[rows:]).astype(BF)
        near = self.ride(self.swap_by_core(near, "xy"), rides[1]).astype(F32)
        return total[:rows] + far[:rows] + near

    def orders(self):
        return [self.near + ["x", "y"], self.near + ["y", "x"]]

    def sequence_gather(self, part, rides=0):
        for bits in zip(*self.orders()):
            came = self.swap_by_core(part, bits)
            if bits[0][0] != "z":
                came = self.ride(came, rides)
            part = jnp.concatenate([part, came], 0)
        return jnp.concatenate([part, self.swap(part, "c")], 0)

    def sequence_scatter(self, part, rides=0):
        rows = part.shape[0] // 2
        part = part[:rows].astype(F32) + self.swap(part[rows:], "c").astype(F32)
        for bits in list(zip(*self.orders()))[::-1]:
            rows = part.shape[0] // 2
            came = self.swap_by_core(part[rows:].astype(BF), bits)
            if bits[0][0] != "z":
                came = self.ride(came, rides)
            part = part[:rows] + came.astype(F32)
        return part

    def owner_orders(self):
        return [["x", "y"] + self.z_bits, ["y", "x"] + self.z_bits]

    def owner_scatter(self, keep, send, rides=0):
        part = keep.astype(F32) + self.swap(send, "c").astype(F32)
        stages = [part]
        for bits in zip(*self.owner_orders()):
            rows = part.shape[1] // 2
            came = self.swap_by_core(part[:, rows:].astype(BF), bits)
            if bits[0][0] != "z":
                came = self.ride(came, rides)
            part = part[:, :rows] + came.astype(F32)
            stages.append(part)
        return stages

    def total(self, value, rows_high):
        for bit in ["c", "x", "y"] + self.z_bits:
            value = value + self.swap(value, bit)
        return lax.psum(value, "rh") if rows_high > 1 else value


def step(
    shape,
    source_bytes,
    decoder_bytes,
    target_bytes,
    target_keep,
    source_length,
    target_length,
    language,
    step_count,
    attn_weights,
    attn_first,
    attn_second,
    feed_weights,
    feed_first,
    feed_second,
    table_weights,
    table_first,
    table_second,
    norm_gain_stack,
    gain_first,
    gain_second,
):
    rows_high, groups = shape
    rows_n, cols_n = 2 * rows_high, 4 * groups
    links = Links(groups)
    core, zc, yc, xc = (lax.axis_index(a) for a in ("c", "z", "y", "x"))
    on_first = core == 0
    tokens = source_bytes.shape[1]
    chunk = attn_weights.shape[2]
    width = attn_weights.shape[3]
    everywhere = ("rh", "c", "z", "y", "x")

    def own_half(value):
        return jnp.where(on_first, value[..., :HALF], value[..., HALF:])

    def other_half(value):
        return jnp.where(on_first, value[..., HALF:], value[..., :HALF])

    def in_order(own, other, axis):
        return jnp.concatenate(
            [jnp.where(on_first, own, other), jnp.where(on_first, other, own)], axis
        )

    def widen(value):
        pad = [(0, 0)] * (value.ndim - 1) + [(0, HALF - value.shape[-1])]
        return jnp.pad(value, pad)

    def spread_features(value):
        split = value.reshape(value.shape[0], rows_high, 2, chunk).transpose(0, 2, 1, 3)
        return widen(split.reshape(value.shape[0], 2, D // 2)).reshape(value.shape[0], WIDE)

    def join_features(value):
        if rows_high == 1:
            return jnp.concatenate([value[:, : D // 2], value[:, HALF : HALF + D // 2]], 1)
        split = value.reshape(value.shape[0], 2, HALF)[:, :, : D // 2]
        split = split.reshape(value.shape[0], 2, rows_high, chunk).transpose(0, 2, 1, 3)
        return split.reshape(value.shape[0], D)

    half = groups // 2
    packed = jnp.concatenate(
        [source_bytes, decoder_bytes, target_bytes, target_keep]
        + [
            jnp.broadcast_to(v[:, None], (1, tokens))
            for v in (source_length, target_length, language, language)
        ],
        0,
    )
    pairs = []
    for c in range(2):
        for k in range(cols_n):
            block = (((k // 4) % half) * 4 + k % 4) * 2 + c
            pairs.append(((k // 4 // half) * cols_n + block, c * cols_n + k))
    packed = lax.ppermute(packed, ("c", "z", "y", "x"), pairs)
    block = (((zc % half) * 2 + yc) * 2 + xc) * 2 + core
    first_pos = block * tokens
    src_limit, tgt_limit, tongue = packed[4, 0], packed[5, 0], packed[6, 0]
    positions = first_pos + jnp.arange(tokens, dtype=jnp.int32)
    weight = ((positions < tgt_limit) & (packed[3] > 0)).astype(F32)
    member = (tongue == jnp.arange(LANES, dtype=jnp.int32)).astype(F32)
    bit_value = {"c": 1, "x": 2, "y": 4}
    for i, bit in enumerate(links.near):
        bit_value[bit] = 8 << i
    masks = []
    for order in links.orders():
        mask = [0]
        for bit in order:
            mask = mask + [m ^ bit_value[bit] for m in mask]
        masks.append(mask)
    masks = np.array([masks[c] + [m ^ 1 for m in masks[1 - c]] for c in range(2)], np.int32)
    firsts = (jnp.where(on_first, masks[0], masks[1]) ^ block) * tokens

    def places(limit):
        return jnp.concatenate([firsts, jnp.stack([limit, first_pos]).astype(jnp.int32)])

    src_places, tgt_places = places(src_limit), places(tgt_limit)

    attn_t = attn_weights.transpose(0, 1, 3, 2)
    table_t = table_weights.transpose(0, 2, 1)

    def gather_tiles(tiles):
        tiles = tiles.astype(BF)
        if rows_high == 1 and tiles.shape[2] < HALF:
            tiles = widen(tiles)
        full = lax.all_gather(tiles[:, None], everywhere, axis=1, tiled=True)
        if rows_high == 1:
            return full.reshape(tiles.shape[0], 2, INNER, HALF)
        full = full.reshape(tiles.shape[0], rows_high, 2, INNER, chunk).transpose(0, 2, 3, 1, 4)
        return widen(full.reshape(tiles.shape[0], 2, INNER, D // 2))

    early_tiles = jnp.concatenate([attn_t[0], table_t[:1]], 0)
    own_counts = (member * jnp.sum(weight))[: HALF - D // 2]
    if rows_high == 1:
        lane_row = jnp.pad(own_counts, (D // 2, 0))[None, None]
        place = lax.broadcasted_iota(jnp.int32, (5, width, 1), 0) + lax.broadcasted_iota(jnp.int32, (5, width, 1), 1)
        early = gather_tiles(widen(early_tiles) + jnp.where(place == 0, lane_row, 0.0))
        counts = jnp.sum(early[0, :, ::width, D // 2 :].astype(F32), axis=(0, 1))
    else:
        early = gather_tiles(early_tiles)
        counts = lax.psum(own_counts, everywhere)
    inverse = 1.0 / (NLANG * jnp.maximum(counts, 1.0))
    token_scale = weight * jnp.sum(member[: HALF - D // 2] * inverse)

    def project(value, matrix):
        return dot_nt(value[:, :HALF], matrix[0]) + dot_nt(value[:, HALF:], matrix[1])

    def unproject(value, matrix):
        return jnp.concatenate([dot_nn(value, matrix[0]), dot_nn(value, matrix[1])], 1)

    hid = FF // cols_n
    hid_half = hid // 2
    period_rows = PERIOD // hid
    period_groups = chunk // period_rows
    lanes_own = HALF if rows_high == 1 else chunk
    shape3 = (period_rows, period_groups, lanes_own)
    spread = (
        lax.broadcasted_iota(jnp.int32, shape3, 2)
        == lax.broadcasted_iota(jnp.int32, shape3, 1) * period_rows
        + lax.broadcasted_iota(jnp.int32, shape3, 0)
    ).astype(BF)
    flat_shape = (6, chunk * hid // LANES, LANES)
    feed_t = unflatten(feed_weights.reshape(flat_shape), spread, hid, period_groups)
    if rows_high > 1:
        feed_t = lax.all_gather(feed_t[None], "rh", axis=0, tiled=True)
        feed_t = widen(feed_t.transpose(1, 2, 0, 3).reshape(6, hid, D // 2))

    def halves_joined(mine):
        keep = jnp.where(on_first, mine[:, :hid_half], mine[:, hid_half:])
        send = jnp.where(on_first, mine[:, hid_half:], mine[:, :hid_half])
        return in_order(keep, links.swap(send, "c"), 2)

    def gather_trip(own, out):
        held = [own]
        for _ in range(groups - 1):
            held.append((yield held[-1], 1))
        out.append(jnp.concatenate(held, 0))

    def scatter_trip(grads, out):
        grads = grads.reshape(groups, hid_half, WIDE)
        value = grads[groups - 1]
        for s in range(groups - 2, -1, -1):
            came = yield value.astype(BF), -1
            value = grads[s].astype(F32) + came.astype(F32)
        out.append(value)

    def collect(outs):
        links.unload()
        return [o[0] for o in outs]

    def to_rows(value):
        keep, send = own_half(value).astype(F32), other_half(value).astype(BF)
        full = in_order(keep, links.swap(send, "c").astype(F32), 1)
        if rows_high > 1:
            full = full[:, :, : D // 2].reshape(3, hid, rows_high, chunk)
            full = lax.psum_scatter(full, "rh", scatter_dimension=2, tiled=True)
            full = full.reshape(3, hid, chunk)
        return full

    late = gather_tiles(jnp.concatenate([attn_t[1], attn_t[2], table_t[1:]], 0))
    weights = [early[:4], late[:4], late[4:8]]
    head_w = late[8]
    own_enc, own_dec = halves_joined(feed_t[:3]), halves_joined(feed_t[3:])
    feed_enc, feed_dec = [[], [], []], [[], [], []]
    links.load(*(gather_trip(own_enc[m], feed_enc[m]) for m in range(3)))
    gains = spread_features(norm_gain_stack)

    def norm(stream, index):
        scale = rms_scale(stream)
        return (stream * scale * gains[index]).astype(BF), scale

    def attention(normed_q, normed_kv, matrices, where, causal, rides):
        queries = project(normed_q, matrices[0]).astype(BF)
        kv = jnp.concatenate([project(normed_kv, matrices[1]), project(normed_kv, matrices[2])], 1)
        kv = links.sequence_gather(kv.astype(BF), rides)
        context = attend(where, queries, kv, causal)
        return unproject(context, matrices[3]), (queries, kv, context)

    def eighths(left, right):
        rows = left[0].shape[0] // 8

        def part_of(first, last):
            at = slice(first * rows, last * rows)
            terms = [dot_nn(a[at], b) for a, b in zip(left, right)]
            return functools.reduce(jnp.add, terms)

        return part_of

    def feed(normed, outs, after=()):
        everyone = links.plane_gather(normed, (1, 1))
        matrices = collect(outs)
        links.load(*after)
        gate = dot_nt(everyone, matrices[0])
        upper = dot_nt(everyone, matrices[1])
        hidden = gated_units(gate, upper).astype(BF)
        out = links.plane_scatter(eighths([hidden], [matrices[2]]), (1, 1))
        return out, (everyone, gate, upper, hidden), matrices

    vocab_ids = jnp.arange(INNER, dtype=jnp.int32)
    src_hot = (packed[0][:, None] == vocab_ids).astype(BF)
    dec_hot = (packed[1][:, None] == vocab_ids).astype(BF)
    embed_w = early[4]
    enc_zero = unproject(src_hot, embed_w)
    dec_zero = unproject(dec_hot, embed_w)
    n_zero, s_zero = norm(links.ride(enc_zero, 2), 0)
    branch, kept_enc = attention(n_zero, n_zero, early[:4], src_places, False, 2)
    enc_one = enc_zero + branch
    n_one, s_one = norm(enc_one, 1)
    branch, kept_enc_feed, feed_enc = feed(
        n_one, feed_enc, (gather_trip(own_dec[m], feed_dec[m]) for m in range(3))
    )
    enc_two = enc_one + branch
    memory, s_two = norm(enc_two, 2)
    n_three, s_three = norm(dec_zero, 3)
    branch, kept_dec = attention(n_three, n_three, weights[1], tgt_places, True, 1)
    dec_one = dec_zero + branch
    n_four, s_four = norm(dec_one, 4)
    branch, kept_cross = attention(n_four, memory, weights[2], src_places, False, 1)
    dec_two = dec_one + branch
    n_five, s_five = norm(dec_two, 5)
    branch, kept_dec_feed, feed_dec = feed(n_five, feed_dec)
    dec_three = dec_two + branch
    final, s_six = norm(dec_three, 6)

    logits = project(final, head_w)
    lse = jax.nn.logsumexp(logits, axis=-1)
    target_hot = (packed[2][:, None] == vocab_ids).astype(F32)
    picked = jnp.sum(logits * target_hot, axis=-1)
    loss_local = jnp.sum((lse - picked) * token_scale)
    grad_logits = ((jnp.exp(logits - lse[:, None]) - target_hot) * token_scale[:, None]).astype(BF)

    own_index = zc * 4 + yc * 2 + xc
    place = {"x": 1, "y": 2}
    for i, bit in enumerate(links.z_bits):
        place[bit] = 4 << i
    relative_masks = []
    for order in links.owner_orders():
        mask = [0]
        for bit in order[::-1]:
            mask = mask + [m ^ place[bit] for m in mask]
        relative_masks.append(np.repeat(np.array(mask, np.int32), width))
    columns = jnp.arange(INNER, dtype=jnp.int32)

    def shuffle_to(mask):
        moved = (mask ^ own_index) * width + columns % width
        return (columns[:, None] == moved[None, :]).astype(BF)

    to_own = shuffle_to(jnp.where(on_first, relative_masks[0], relative_masks[1]))
    to_other = shuffle_to(jnp.where(on_first, relative_masks[1], relative_masks[0]))

    def owner_grads(pairs, rides=0):
        tokens_n = max(p[0].shape[0] for p in pairs)

        def filled(value):
            return jnp.pad(value, ((0, tokens_n - value.shape[0]), (0, 0)))

        cols = jnp.concatenate([filled(p[0]) for p in pairs], 0)
        batch = (((1,), (1,)), ((0,), (0,)))

        def products(shuffle, half_of):
            moved = dot_nn(cols, shuffle).astype(BF).reshape(len(pairs), tokens_n, INNER)
            feats = jnp.stack([filled(half_of(p[1])) for p in pairs])
            return lax.dot_general(moved, feats, batch, preferred_element_type=F32).astype(BF)

        return links.owner_scatter(products(to_own, own_half), products(to_other, other_half), rides)

    def feed_back(kept, matrices, grad, events=((), ()), rides=((0, 0), (0, 0))):
        everyone, gate, upper, hidden = kept
        grad_all = anchor(links.plane_gather(grad.astype(BF), rides[0]), *events[0])
        _, pull = jax.vjp(gated_units, gate, upper)
        grad_gate, grad_upper = pull(dot_nt(grad_all, matrices[2]))
        gate_b, upper_b = grad_gate.astype(BF), grad_upper.astype(BF)
        grad_normed = anchor(links.plane_scatter(eighths([gate_b, upper_b], matrices[:2]), rides[1]), *events[1])
        grads = [
            dot_tn(gate_b, everyone).astype(BF),
            dot_tn(upper_b, everyone).astype(BF),
            dot_tn(hidden, grad_all).astype(BF),
        ]
        return grad_normed, grads

    def attention_back(kept, normed_q, normed_kv, matrices, where, causal, grad, rides=0, events=((), ())):
        queries, kv, context = kept
        grad_b = grad.astype(BF)
        grad_context = anchor(project(grad_b, matrices[3]).astype(BF), *events[0])
        d_query, d_kv = attend_back(where, queries, grad_context, kv, causal)
        d_kv = anchor(d_kv, *events[1])
        d_kv_own = links.sequence_scatter(d_kv, rides).astype(BF)
        d_key, d_value = d_kv_own[:, :INNER], d_kv_own[:, INNER:]
        d_normed_q = unproject(d_query, matrices[0])
        d_normed_kv = unproject(d_key, matrices[1]) + unproject(d_value, matrices[2])
        pairs = [(d_query, normed_q), (d_key, normed_kv), (d_value, normed_kv), (context, grad_b)]
        return d_normed_q, d_normed_kv, pairs

    grad_final = unproject(grad_logits, head_w)
    grad_dec, gain_six = rms_reverse(dec_three, gains[6], s_six, grad_final)
    grad_normed, feed_dec_grad = feed_back(kept_dec_feed, feed_dec, grad_dec)
    part, gain_five = rms_reverse(dec_two, gains[5], s_five, grad_normed)
    grad_dec = grad_dec + part
    dec_feed, enc_feed = [[], [], []], [[], [], []]
    links.load(*(scatter_trip(feed_dec_grad[m], dec_feed[m]) for m in range(3)))
    d_q, grad_memory, cross_grad = attention_back(
        kept_cross, n_four, memory, weights[2], src_places, False, grad_dec, 2
    )
    cross_stages = owner_grads(cross_grad + [(grad_logits, final)])
    part, gain_four = rms_reverse(dec_one, gains[4], s_four, d_q)
    grad_dec = grad_dec + part
    d_q, d_kv, dec_grad = attention_back(
        kept_dec, n_three, n_three, weights[1], tgt_places, True, grad_dec
    )
    dec_stages = owner_grads(dec_grad)
    part, gain_three = rms_reverse(dec_zero, gains[3], s_three, d_q + d_kv)
    grad_dec = grad_dec + part
    grad_enc, gain_two = rms_reverse(enc_two, gains[2], s_two, grad_memory)
    grad_normed, feed_enc_grad = feed_back(
        kept_enc_feed, feed_enc, grad_enc, ((cross_stages[0],), (cross_stages[1], dec_stages[0])), ((1, 1), (2, 1))
    )
    part, gain_one = rms_reverse(enc_one, gains[1], s_one, grad_normed)
    grad_enc = grad_enc + part
    links.unload()
    dec_rows = to_rows(jnp.stack([o[0] for o in dec_feed]))
    dec_flat = flatten(dec_rows, spread, hid, period_groups)
    links.load(*(scatter_trip(feed_enc_grad[m], enc_feed[m]) for m in range(3)))
    d_q, d_kv, enc_grad = attention_back(
        kept_enc, n_zero, n_zero, weights[0], src_places, False, grad_enc, 2,
        ((cross_stages[2], dec_stages[1]), (cross_stages[3], dec_stages[2], dec_flat)),
    )
    part, gain_zero = rms_reverse(enc_zero, gains[0], s_zero, d_q + d_kv)
    grad_enc = grad_enc + part
    embed_pair = (
        jnp.concatenate([src_hot, dec_hot], 0),
        jnp.concatenate([grad_enc, grad_dec], 0).astype(BF),
    )

    early_stages = owner_grads(enc_grad + [embed_pair], 2)
    links.unload()

    def own_chunk(value):
        if rows_high > 1:
            value = value[:, :, : D // 2].reshape(value.shape[0], width, rows_high, chunk)
            value = lax.psum_scatter(value, "rh", scatter_dimension=2, tiled=True)
            value = value.reshape(value.shape[0], width, chunk)
        return value

    enc_rows = to_rows(jnp.stack([o[0] for o in enc_feed]))
    enc_flat = flatten(enc_rows, spread, hid, period_groups)
    early_red = own_chunk(early_stages[-1])
    dec_red, cross_red = own_chunk(dec_stages[-1]), own_chunk(cross_stages[-1])
    square_local = functools.reduce(
        jnp.add, [jnp.sum(v * v) for v in (early_red, dec_red, cross_red, enc_rows, dec_rows)]
    )
    lane = jnp.arange(WIDE)
    extra = jnp.where(lane == 0, square_local, 0.0) + jnp.where(lane == 1, loss_local, 0.0)
    gain_local = jnp.stack(
        [gain_zero, gain_one, gain_two, gain_three, gain_four, gain_five, gain_six, extra]
    )
    gain_local = anchor(gain_local, enc_flat, dec_flat)
    everything = links.total(gain_local, rows_high)
    loss = everything[7, 1]
    grad_norm = jnp.sqrt(everything[7, 0] + jnp.sum(everything[:7] * everything[:7]))
    count = step_count[0].astype(F32)
    scalars = jnp.stack([1.0 / (1.0 - BETA_FIRST**count), 1.0 / (1.0 - BETA_SECOND**count)])
    slot_total = tokens * cols_n

    def attn_turn(value):
        return value.transpose(0, 1, 3, 2).reshape(12, width, chunk)

    def attn_return(value):
        return value.reshape(3, 4, width, chunk).transpose(0, 1, 3, 2)

    def table_turn(value):
        return value.transpose(0, 2, 1)

    new = finish(
        (slot_total / (3.0 * INNER)) ** 0.5,
        scalars,
        everything,
        (enc_flat, dec_flat),
        (early_red, dec_red, cross_red, join_features(everything[:7])),
        tuple(v.reshape(flat_shape) for v in (feed_weights, feed_first, feed_second)),
        tuple(attn_turn(v) for v in (attn_weights, attn_first, attn_second)),
        tuple(table_turn(v) for v in (table_weights, table_first, table_second)),
        (norm_gain_stack, gain_first, gain_second),
    )
    return (
        (loss, grad_norm)
        + tuple(attn_return(v) for v in new[3:6])
        + tuple(v.reshape(feed_weights.shape) for v in new[:3])
        + tuple(table_turn(v) for v in new[6:9])
        + tuple(new[9:])
    )


def solution(mesh):
    rows_high = mesh.shape["row"] // 2
    groups = mesh.shape["col"] // 4
    split = Mesh(mesh.devices.reshape(rows_high, 2, groups, 2, 2), ("rh", "c", "z", "y", "x"))
    row, col = ("rh", "c"), ("z", "y", "x")
    attn = P(None, None, row, col)
    feed = P(None, None, col, row)
    table = P(None, row, col)
    ids = P(row, col)
    in_specs = (ids,) * 4 + (P(row),) * 3 + (P(),) + (attn,) * 3 + (feed,) * 3 + (table,) * 3 + (P(),) * 3
    out_specs = (P(), P()) + (attn,) * 3 + (feed,) * 3 + (table,) * 3 + (P(),) * 3
    return jax.shard_map(
        functools.partial(step, (rows_high, groups)),
        mesh=split,
        in_specs=in_specs,
        out_specs=out_specs,
        check_vma=False,
    )
```

```python
import functools

import jax
import jax.numpy as jnp
import numpy as np
from jax import lax
from jax.experimental import pallas as pl
from jax.experimental.pallas import tpu as pltpu
from jax.sharding import Mesh, PartitionSpec as P

D = 1472
HEADS = 6
HEAD_DIM = 64
NLANG = 4
INNER = 384
FF = 3584
LANES = 128
HALF = 768
WIDE = 2 * HALF

RMS_EPS = 1e-06
CLIP_NORM = 0.01
BETA_FIRST = 0.9
BETA_SECOND = 0.999
ADAM_EPS = 1e-08
MATRIX_RATE = 0.05
GAIN_RATE = 0.2
DECAY_STEP = 0.005
MASKED = -1000000000.0
PERIOD = 896
MIB = 1024 * 1024
BF = jnp.bfloat16
F32 = jnp.float32


def dot_nn(a, b):
    return lax.dot_general(a, b, (((1,), (0,)), ((), ())), preferred_element_type=F32)


def dot_nt(a, b):
    return lax.dot_general(a, b, (((1,), (1,)), ((), ())), preferred_element_type=F32)


def dot_tn(a, b):
    return lax.dot_general(a, b, (((0,), (0,)), ((), ())), preferred_element_type=F32)


def flat_pieces(hid):
    found = []
    for t in range(PERIOD // LANES):
        at = LANES * t
        while at < LANES * (t + 1):
            j = at // hid
            end = min(LANES * (t + 1), (j + 1) * hid)
            found.append((t, at - LANES * t, j, at - j * hid, end - at))
            at = end
    return found


def unflatten_kernel(hid, groups, flat_ref, spread_ref, out_ref, acc_ref):
    chunks = PERIOD // LANES
    acc_ref[...] = jnp.zeros_like(acc_ref)
    for t in range(chunks):
        rows = flat_ref[0, pl.ds(t, groups, stride=chunks), :].astype(BF)
        for piece_t, lane, j, first, length in flat_pieces(hid):
            if piece_t == t:
                placed = dot_tn(rows, spread_ref[j])
                acc_ref[first : first + length, :] += placed[lane : lane + length, :]
    out_ref[0] = acc_ref[...].astype(BF)


def unflatten(flat, spread, hid, groups):
    count, flat_rows, _ = flat.shape
    lanes = spread.shape[2]
    return pl.pallas_call(
        functools.partial(unflatten_kernel, hid, groups),
        out_shape=jax.ShapeDtypeStruct((count, hid, lanes), BF),
        grid=(count,),
        in_specs=[
            pl.BlockSpec((1, flat_rows, LANES), lambda i: (i, 0, 0)),
            pl.BlockSpec(spread.shape, lambda i: (0, 0, 0)),
        ],
        out_specs=pl.BlockSpec((1, hid, lanes), lambda i: (i, 0, 0)),
        scratch_shapes=[pltpu.VMEM((hid, lanes), F32)],
        compiler_params=pltpu.CompilerParams(vmem_limit_bytes=10 * MIB),
        name="unflatten",
    )(flat, spread)


def flatten_kernel(hid, groups, grad_ref, spread_ref, out_ref):
    chunks = PERIOD // LANES
    grads = grad_ref[0].astype(BF)
    for t in range(chunks):
        total = jnp.zeros((groups, LANES), F32)
        for piece_t, lane, j, first, length in flat_pieces(hid):
            if piece_t == t:
                rows = grads[first : first + length, :]
                parts = []
                if lane > 0:
                    parts.append(jnp.zeros((lane, rows.shape[1]), BF))
                parts.append(rows)
                if lane + length < LANES:
                    parts.append(jnp.zeros((LANES - lane - length, rows.shape[1]), BF))
                rows = jnp.concatenate(parts, 0) if len(parts) > 1 else rows
                total = total + dot_nt(spread_ref[j], rows)
        out_ref[0, pl.ds(t, groups, stride=chunks), :] = total


def flatten(grads, spread, hid, groups):
    count, _, lanes = grads.shape
    flat_rows = groups * PERIOD // LANES
    return pl.pallas_call(
        functools.partial(flatten_kernel, hid, groups),
        out_shape=jax.ShapeDtypeStruct((count, flat_rows, LANES), F32),
        grid=(count,),
        in_specs=[
            pl.BlockSpec((1, hid, lanes), lambda i: (i, 0, 0)),
            pl.BlockSpec(spread.shape, lambda i: (0, 0, 0)),
        ],
        out_specs=pl.BlockSpec((1, flat_rows, LANES), lambda i: (i, 0, 0)),
        compiler_params=pltpu.CompilerParams(vmem_limit_bytes=10 * MIB),
        name="flatten",
    )(grads, spread)


def finish_kernel(
    slot_rate, scal_ref, all_ref, enc_ref, dec_ref, early_ref, own_ref, cross_ref, gain_ref,
    fw_ref, fm_ref, fv_ref, aw_ref, am_ref, av_ref, tw_ref, tm_ref, tv_ref, gw_ref, gm_ref, gv_ref,
    fm_out, fv_out, fw_out, am_out, av_out, aw_out, tm_out, tv_out, tw_out, gm_out, gv_out, gw_out,
):
    at = pl.program_id(0)
    gains = all_ref[0:7, :]
    square = jnp.sum(jnp.sum(gains * gains, axis=1, keepdims=True), axis=0, keepdims=True)
    norm = jnp.sqrt(all_ref[7:8, 0:1] + square)
    clip = CLIP_NORM / jnp.maximum(norm, CLIP_NORM)
    scales = (clip, scal_ref[0], scal_ref[1])

    def feed(grad_ref):
        fm_out[0], fv_out[0], fw_out[0] = adam_rule(
            fw_ref[0], fm_ref[0], fv_ref[0], grad_ref[0], *scales, MATRIX_RATE, DECAY_STEP
        )

    @pl.when(at < 3)
    def _():
        feed(enc_ref)

    @pl.when(at >= 3)
    def _():
        feed(dec_ref)

    chunk = aw_ref.shape[2]
    grads = [ref.at[i] for ref in (early_ref, own_ref, cross_ref) for i in range(4)]
    for i, grad in enumerate(grads):

        @pl.when(at == i // 2)
        def _(i=i, grad=grad):
            rate = slot_rate if i % 4 == 3 else MATRIX_RATE
            k = i % 2
            am_out[k], av_out[k], aw_out[k] = adam_rule(
                aw_ref[k], am_ref[k], av_ref[k], grad[:, :chunk], *scales, rate, DECAY_STEP
            )

    @pl.when(at == 5)
    def _():
        for i, (grad, rate) in enumerate(((early_ref.at[4], 1.0), (cross_ref.at[4], 1.5 * D ** (-0.5)))):
            tm_out[i], tv_out[i], tw_out[i] = adam_rule(
                tw_ref[i], tm_ref[i], tv_ref[i], grad[:, :chunk], *scales, rate, DECAY_STEP
            )
        gm_out[...], gv_out[...], gw_out[...] = adam_rule(
            gw_ref[...], gm_ref[...], gv_ref[...], gain_ref[...], *scales, GAIN_RATE, 0.0
        )


def finish(slot_rate, scalars, everything, feed_grads, rest_grads, feed, attn, table, gain):
    block = (1,) + feed[0].shape[1:]
    flat = pl.BlockSpec(block, lambda i: (i, 0, 0))

    def whole(value):
        return pl.BlockSpec(value.shape, lambda i: (0,) * value.ndim)

    def like(value):
        return jax.ShapeDtypeStruct(value.shape, F32)

    rest = table + gain
    pair = pl.BlockSpec((2,) + attn[0].shape[1:], lambda i: (i, 0, 0))
    return pl.pallas_call(
        functools.partial(finish_kernel, slot_rate),
        out_shape=[like(v) for v in feed + attn + rest],
        grid=(6,),
        in_specs=[pl.BlockSpec(memory_space=pltpu.SMEM), whole(everything)]
        + [
            pl.BlockSpec(block, lambda i: (jnp.minimum(i, 2), 0, 0)),
            pl.BlockSpec(block, lambda i: (jnp.maximum(i - 3, 0), 0, 0)),
        ]
        + [whole(v) for v in rest_grads]
        + [flat] * 3
        + [pair] * 3
        + [whole(v) for v in rest],
        out_specs=[flat] * 3 + [pair] * 3 + [whole(v) for v in rest],
        compiler_params=pltpu.CompilerParams(vmem_limit_bytes=56 * MIB),
        name="finish",
    )(scalars, everything, *feed_grads, *rest_grads, *feed, *attn, *rest)


def head_lanes(shape, h):
    lane = lax.broadcasted_iota(jnp.int32, shape, 1)
    return (lane < HEAD_DIM) if h == 0 else (lane >= HEAD_DIM)


def attend_kernel(causal, where_ref, q_ref, kv_ref, out_ref, pos_ref):
    count = q_ref.shape[0]
    length = kv_ref.shape[0]
    blocks = length // count
    limit = where_ref[blocks]
    first = where_ref[blocks + 1]
    for b in range(blocks):
        pos_ref[:, b * count : (b + 1) * count] = (
            lax.broadcasted_iota(jnp.int32, (8, count), 1) + where_ref[b]
        )
    pos = pos_ref[0:1, :]
    last = jnp.full((count, 1), limit - 1, jnp.int32)
    if causal:
        last = jnp.minimum(last, first + lax.broadcasted_iota(jnp.int32, (count, 1), 0))
    allowed = pos <= last
    for p in range(3):
        lanes = slice(p * LANES, (p + 1) * LANES)
        values = slice(INNER + p * LANES, INNER + (p + 1) * LANES)
        queries = q_ref[:, lanes] * HEAD_DIM ** (-0.5)
        context = []
        for h in range(2):
            own = jnp.where(head_lanes(queries.shape, h), queries, jnp.zeros_like(queries))
            scores = dot_nt(own, kv_ref[:, lanes])
            scores = jnp.where(allowed, scores, MASKED)
            raised = jnp.exp(scores - jnp.max(scores, axis=1, keepdims=True))
            probs = raised * (1.0 / jnp.sum(raised, axis=1, keepdims=True))
            context.append(dot_nn(probs.astype(BF), kv_ref[:, values]))
        out_ref[:, lanes] = jnp.where(
            head_lanes(context[0].shape, 0), context[0], context[1]
        ).astype(BF)


def attend(where, queries, kv, causal):
    count = queries.shape[0]
    length = kv.shape[0]
    vmem = pl.BlockSpec(memory_space=pltpu.VMEM)
    return pl.pallas_call(
        functools.partial(attend_kernel, causal),
        out_shape=jax.ShapeDtypeStruct((count, INNER), BF),
        in_specs=[pl.BlockSpec(memory_space=pltpu.SMEM)] + [vmem] * 2,
        out_specs=vmem,
        scratch_shapes=[pltpu.VMEM((8, length), jnp.int32)],
        compiler_params=pltpu.CompilerParams(vmem_limit_bytes=8 * MIB + 4096 * length),
        cost_estimate=pl.CostEstimate(
            flops=4 * count * length * INNER * 2,
            transcendentals=HEADS * count * length,
            bytes_accessed=4 * length * INNER,
        ),
        name="attend",
    )(where, queries, kv)


def attend_back_kernel(causal, where_ref, q_ref, g_ref, kv_ref, dq_ref, dkv_ref, pos_ref):
    count = q_ref.shape[0]
    length = kv_ref.shape[0]
    blocks = length // count
    limit = where_ref[blocks]
    first = where_ref[blocks + 1]
    scale = HEAD_DIM ** (-0.5)
    last = jnp.full((1, count), limit - 1, jnp.int32)
    if causal:
        last = jnp.minimum(last, first + lax.broadcasted_iota(jnp.int32, (1, count), 1))
    for b in range(blocks):
        pos_ref[b * count : (b + 1) * count, :] = (
            lax.broadcasted_iota(jnp.int32, (count, count), 0) + where_ref[b]
        )
    for p in range(3):
        lanes = slice(p * LANES, (p + 1) * LANES)
        values = slice(INNER + p * LANES, INNER + (p + 1) * LANES)
        allowed = pos_ref[...] <= last
        queries = q_ref[:, lanes] * scale
        grads = g_ref[:, lanes]
        d_query, d_key, d_value = [], None, None
        for h in range(2):
            own_q = jnp.where(head_lanes(queries.shape, h), queries, jnp.zeros_like(queries))
            own_g = jnp.where(head_lanes(grads.shape, h), grads, jnp.zeros_like(grads))
            scores = dot_nt(kv_ref[:, lanes], own_q)
            scores = jnp.where(allowed, scores, MASKED)
            raised = jnp.exp(scores - jnp.max(scores, axis=0, keepdims=True))
            probs = raised * (1.0 / jnp.sum(raised, axis=0, keepdims=True))
            d_probs = dot_nt(kv_ref[:, values], own_g)
            inner = jnp.sum(probs * d_probs, axis=0, keepdims=True)
            d_scores = (probs * (d_probs - inner)).astype(BF)
            d_query.append(dot_tn(d_scores, kv_ref[:, lanes]) * scale)
            key_part = dot_nn(d_scores, own_q)
            value_part = dot_nn(probs.astype(BF), own_g)
            d_key = key_part if h == 0 else d_key + key_part
            d_value = value_part if h == 0 else d_value + value_part
        dq_ref[:, lanes] = jnp.where(
            head_lanes(d_query[0].shape, 0), d_query[0], d_query[1]
        ).astype(BF)
        dkv_ref[:, lanes] = d_key.astype(BF)
        dkv_ref[:, values] = d_value.astype(BF)


def attend_back(where, queries, grads, kv, causal):
    count = queries.shape[0]
    length = kv.shape[0]
    vmem = pl.BlockSpec(memory_space=pltpu.VMEM)
    return pl.pallas_call(
        functools.partial(attend_back_kernel, causal),
        out_shape=(
            jax.ShapeDtypeStruct((count, INNER), BF),
            jax.ShapeDtypeStruct((length, 2 * INNER), BF),
        ),
        in_specs=[pl.BlockSpec(memory_space=pltpu.SMEM)] + [vmem] * 3,
        out_specs=(vmem,) * 2,
        scratch_shapes=[pltpu.VMEM((length, count), jnp.int32)],
        compiler_params=pltpu.CompilerParams(vmem_limit_bytes=8 * MIB + 8192 * length),
        cost_estimate=pl.CostEstimate(
            flops=10 * count * length * INNER * 2,
            transcendentals=HEADS * count * length,
            bytes_accessed=8 * length * INNER,
        ),
        name="attend_back",
    )(where, queries, grads, kv)


def rms_scale(stream):
    return lax.rsqrt(jnp.sum(stream * stream, axis=-1, keepdims=True) * (1.0 / D) + RMS_EPS)


def rms_reverse(stream, gain, scale, grad_out):
    weighted = grad_out * gain
    inner_mean = jnp.sum(weighted * stream, axis=-1, keepdims=True) * (1.0 / D)
    grad_in = scale * weighted - stream * (scale * scale * scale) * inner_mean
    grad_gain = jnp.sum(grad_out * stream * scale, axis=0)
    return (grad_in, grad_gain)


def gated_units(gate, upper):
    return jax.nn.gelu(gate, approximate=True) * upper


def adam_rule(weight, first, second, grad, clip, first_scale, second_scale, rate, decay_step):
    clipped = grad * clip
    first_new = BETA_FIRST * first + (1.0 - BETA_FIRST) * clipped
    second_new = BETA_SECOND * second + (1.0 - BETA_SECOND) * clipped * clipped
    ratio = first_new * first_scale / (jnp.sqrt(second_new * second_scale) + ADAM_EPS)
    return (first_new, second_new, weight - rate * ratio - decay_step * weight)


def anchor(value, *events):
    return lax.optimization_barrier((value,) + events)[0] if events else value


class Links:
    def __init__(self, groups):
        self.groups = groups
        self.z_bits = [f"z{i}" for i in range(groups.bit_length() - 1)]
        self.near = self.z_bits[:-1] if len(self.z_bits) > 1 else []
        self.cargo = []

    def load(self, *trips):
        self.cargo += [(trip, next(trip)) for trip in trips]

    def ship(self):
        trip, (value, step) = self.cargo.pop(0)
        return trip, self.ring(value, step)

    def land(self, trip, came):
        try:
            self.cargo.insert(min(1, len(self.cargo)), (trip, trip.send(came)))
        except StopIteration:
            pass

    def ride(self, value, count=1):
        sent = [self.ship() for _ in range(min(count, len(self.cargo)))]
        if sent:
            came = lax.optimization_barrier((value,) + tuple(c for _, c in sent))
            value = came[0]
            for (trip, _), c in zip(sent, came[1:]):
                self.land(trip, c)
        return value

    def unload(self):
        while self.cargo:
            self.land(*self.ship())

    def swap(self, value, bit):
        if bit[0] == "z":
            step = 1 << int(bit[1:])
            return lax.ppermute(value, "z", [(i, i ^ step) for i in range(self.groups)])
        return lax.ppermute(value, bit, [(0, 1), (1, 0)])

    def swap_by_core(self, value, bits):
        chips = 4 * self.groups
        masks = {"x": 1, "y": 2}
        for i, bit in enumerate(self.z_bits):
            masks[bit] = 4 << i
        pairs = [(c * chips + k, c * chips + (k ^ masks[bits[c]])) for c in range(2) for k in range(chips)]
        return lax.ppermute(value, ("c", "z", "y", "x"), pairs)

    def ring(self, value, step):
        n = self.groups
        return lax.ppermute(value, "z", [(i, (i + step) % n) for i in range(n)])

    def plane_gather(self, own, rides=(0, 0)):
        first = self.ride(self.swap_by_core(own, "xy"), rides[0])
        pair = jnp.concatenate([own, first], 0)
        second = self.ride(self.swap_by_core(pair, "yx"), rides[1])
        mine = jnp.concatenate([pair, second], 0)
        return jnp.concatenate([mine, self.swap(mine, "c")], 0)

    def plane_scatter(self, part_of, rides=(0, 0)):
        total = self.swap(part_of(4, 8).astype(BF), "c").astype(F32) + part_of(0, 4)
        rows = total.shape[0] // 4
        far = self.ride(self.swap_by_core(total[2 * rows :].astype(BF), "yx"), rides[0]).astype(F32)
        near = (total[rows : 2 * rows] + far[rows:]).astype(BF)
        near = self.ride(self.swap_by_core(near, "xy"), rides[1]).astype(F32)
        return total[:rows] + far[:rows] + near

    def orders(self):
        return [self.near + ["x", "y"], self.near + ["y", "x"]]

    def sequence_gather(self, part, rides=0):
        for bits in zip(*self.orders()):
            came = self.swap_by_core(part, bits)
            if bits[0][0] != "z":
                came = self.ride(came, rides)
            part = jnp.concatenate([part, came], 0)
        return jnp.concatenate([part, self.swap(part, "c")], 0)

    def sequence_scatter(self, part, rides=0):
        rows = part.shape[0] // 2
        part = part[:rows].astype(F32) + self.swap(part[rows:], "c").astype(F32)
        for bits in list(zip(*self.orders()))[::-1]:
            rows = part.shape[0] // 2
            came = self.swap_by_core(part[rows:].astype(BF), bits)
            if bits[0][0] != "z":
                came = self.ride(came, rides)
            part = part[:rows] + came.astype(F32)
        return part

    def owner_orders(self):
        return [["x", "y"] + self.z_bits, ["y", "x"] + self.z_bits]

    def owner_scatter(self, keep, send, rides=0):
        part = keep.astype(F32) + self.swap(send, "c").astype(F32)
        stages = [part]
        for bits in zip(*self.owner_orders()):
            rows = part.shape[1] // 2
            came = self.swap_by_core(part[:, rows:].astype(BF), bits)
            if bits[0][0] != "z":
                came = self.ride(came, rides)
            part = part[:, :rows] + came.astype(F32)
            stages.append(part)
        return stages

    def total(self, value, rows_high):
        for bit in ["c", "x", "y"] + self.z_bits:
            value = value + self.swap(value, bit)
        return lax.psum(value, "rh") if rows_high > 1 else value


def step(
    shape,
    source_bytes,
    decoder_bytes,
    target_bytes,
    target_keep,
    source_length,
    target_length,
    language,
    step_count,
    attn_weights,
    attn_first,
    attn_second,
    feed_weights,
    feed_first,
    feed_second,
    table_weights,
    table_first,
    table_second,
    norm_gain_stack,
    gain_first,
    gain_second,
):
    rows_high, groups = shape
    rows_n, cols_n = 2 * rows_high, 4 * groups
    links = Links(groups)
    core, zc, yc, xc = (lax.axis_index(a) for a in ("c", "z", "y", "x"))
    on_first = core == 0
    tokens = source_bytes.shape[1]
    chunk = attn_weights.shape[2]
    width = attn_weights.shape[3]
    everywhere = ("rh", "c", "z", "y", "x")

    def own_half(value):
        return jnp.where(on_first, value[..., :HALF], value[..., HALF:])

    def other_half(value):
        return jnp.where(on_first, value[..., HALF:], value[..., :HALF])

    def in_order(own, other, axis):
        return jnp.concatenate(
            [jnp.where(on_first, own, other), jnp.where(on_first, other, own)], axis
        )

    def widen(value):
        pad = [(0, 0)] * (value.ndim - 1) + [(0, HALF - value.shape[-1])]
        return jnp.pad(value, pad)

    def spread_features(value):
        split = value.reshape(value.shape[0], rows_high, 2, chunk).transpose(0, 2, 1, 3)
        return widen(split.reshape(value.shape[0], 2, D // 2)).reshape(value.shape[0], WIDE)

    def join_features(value):
        if rows_high == 1:
            return jnp.concatenate([value[:, : D // 2], value[:, HALF : HALF + D // 2]], 1)
        split = value.reshape(value.shape[0], 2, HALF)[:, :, : D // 2]
        split = split.reshape(value.shape[0], 2, rows_high, chunk).transpose(0, 2, 1, 3)
        return split.reshape(value.shape[0], D)

    half = groups // 2
    packed = jnp.concatenate(
        [source_bytes, decoder_bytes, target_bytes, target_keep]
        + [
            jnp.broadcast_to(v[:, None], (1, tokens))
            for v in (source_length, target_length, language, language)
        ],
        0,
    )
    pairs = []
    for c in range(2):
        for k in range(cols_n):
            block = (((k // 4) % half) * 4 + k % 4) * 2 + c
            pairs.append(((k // 4 // half) * cols_n + block, c * cols_n + k))
    packed = lax.ppermute(packed, ("c", "z", "y", "x"), pairs)
    block = (((zc % half) * 2 + yc) * 2 + xc) * 2 + core
    first_pos = block * tokens
    src_limit, tgt_limit, tongue = packed[4, 0], packed[5, 0], packed[6, 0]
    positions = first_pos + jnp.arange(tokens, dtype=jnp.int32)
    weight = ((positions < tgt_limit) & (packed[3] > 0)).astype(F32)
    member = (tongue == jnp.arange(LANES, dtype=jnp.int32)).astype(F32)
    bit_value = {"c": 1, "x": 2, "y": 4}
    for i, bit in enumerate(links.near):
        bit_value[bit] = 8 << i
    masks = []
    for order in links.orders():
        mask = [0]
        for bit in order:
            mask = mask + [m ^ bit_value[bit] for m in mask]
        masks.append(mask)
    masks = np.array([masks[c] + [m ^ 1 for m in masks[1 - c]] for c in range(2)], np.int32)
    firsts = (jnp.where(on_first, masks[0], masks[1]) ^ block) * tokens

    def places(limit):
        return jnp.concatenate([firsts, jnp.stack([limit, first_pos]).astype(jnp.int32)])

    src_places, tgt_places = places(src_limit), places(tgt_limit)

    attn_t = attn_weights.transpose(0, 1, 3, 2)
    table_t = table_weights.transpose(0, 2, 1)

    def gather_tiles(tiles):
        tiles = tiles.astype(BF)
        if rows_high == 1 and tiles.shape[2] < HALF:
            tiles = widen(tiles)
        full = lax.all_gather(tiles[:, None], everywhere, axis=1, tiled=True)
        if rows_high == 1:
            return full.reshape(tiles.shape[0], 2, INNER, HALF)
        full = full.reshape(tiles.shape[0], rows_high, 2, INNER, chunk).transpose(0, 2, 3, 1, 4)
        return widen(full.reshape(tiles.shape[0], 2, INNER, D // 2))

    early_tiles = jnp.concatenate([attn_t[0], table_t[:1]], 0)
    own_counts = (member * jnp.sum(weight))[: HALF - D // 2]
    if rows_high == 1:
        lane_row = jnp.pad(own_counts, (D // 2, 0))[None, None]
        place = lax.broadcasted_iota(jnp.int32, (5, width, 1), 0) + lax.broadcasted_iota(jnp.int32, (5, width, 1), 1)
        early = gather_tiles(widen(early_tiles) + jnp.where(place == 0, lane_row, 0.0))
        counts = jnp.sum(early[0, :, ::width, D // 2 :].astype(F32), axis=(0, 1))
    else:
        early = gather_tiles(early_tiles)
        counts = lax.psum(own_counts, everywhere)
    inverse = 1.0 / (NLANG * jnp.maximum(counts, 1.0))
    token_scale = weight * jnp.sum(member[: HALF - D // 2] * inverse)

    def project(value, matrix):
        return dot_nt(value[:, :HALF], matrix[0]) + dot_nt(value[:, HALF:], matrix[1])

    def unproject(value, matrix):
        return jnp.concatenate([dot_nn(value, matrix[0]), dot_nn(value, matrix[1])], 1)

    hid = FF // cols_n
    hid_half = hid // 2
    period_rows = PERIOD // hid
    period_groups = chunk // period_rows
    lanes_own = HALF if rows_high == 1 else chunk
    shape3 = (period_rows, period_groups, lanes_own)
    spread = (
        lax.broadcasted_iota(jnp.int32, shape3, 2)
        == lax.broadcasted_iota(jnp.int32, shape3, 1) * period_rows
        + lax.broadcasted_iota(jnp.int32, shape3, 0)
    ).astype(BF)
    flat_shape = (6, chunk * hid // LANES, LANES)
    feed_t = unflatten(feed_weights.reshape(flat_shape), spread, hid, period_groups)
    if rows_high > 1:
        feed_t = lax.all_gather(feed_t[None], "rh", axis=0, tiled=True)
        feed_t = widen(feed_t.transpose(1, 2, 0, 3).reshape(6, hid, D // 2))

    def halves_joined(mine):
        keep = jnp.where(on_first, mine[:, :hid_half], mine[:, hid_half:])
        send = jnp.where(on_first, mine[:, hid_half:], mine[:, :hid_half])
        return in_order(keep, links.swap(send, "c"), 2)

    def gather_trip(own, out):
        held = [own]
        for _ in range(groups - 1):
            held.append((yield held[-1], 1))
        out.append(jnp.concatenate(held, 0))

    def scatter_trip(grads, out):
        grads = grads.reshape(groups, hid_half, WIDE)
        value = grads[groups - 1]
        for s in range(groups - 2, -1, -1):
            came = yield value.astype(BF), -1
            value = grads[s].astype(F32) + came.astype(F32)
        out.append(value)

    def collect(outs):
        links.unload()
        return [o[0] for o in outs]

    def to_rows(value):
        keep, send = own_half(value).astype(F32), other_half(value).astype(BF)
        full = in_order(keep, links.swap(send, "c").astype(F32), 1)
        if rows_high > 1:
            full = full[:, :, : D // 2].reshape(3, hid, rows_high, chunk)
            full = lax.psum_scatter(full, "rh", scatter_dimension=2, tiled=True)
            full = full.reshape(3, hid, chunk)
        return full

    late = gather_tiles(jnp.concatenate([attn_t[1], attn_t[2], table_t[1:]], 0))
    weights = [early[:4], late[:4], late[4:8]]
    head_w = late[8]
    own_enc, own_dec = halves_joined(feed_t[:3]), halves_joined(feed_t[3:])
    feed_enc, feed_dec = [[], [], []], [[], [], []]
    links.load(*(gather_trip(own_enc[m], feed_enc[m]) for m in range(3)))
    gains = spread_features(norm_gain_stack)

    def norm(stream, index):
        scale = rms_scale(stream)
        return (stream * scale * gains[index]).astype(BF), scale

    def attention(normed_q, normed_kv, matrices, where, causal, rides):
        queries = project(normed_q, matrices[0]).astype(BF)
        kv = jnp.concatenate([project(normed_kv, matrices[1]), project(normed_kv, matrices[2])], 1)
        kv = links.sequence_gather(kv.astype(BF), rides)
        context = attend(where, queries, kv, causal)
        return unproject(context, matrices[3]), (queries, kv, context)

    def eighths(left, right):
        rows = left[0].shape[0] // 8

        def part_of(first, last):
            at = slice(first * rows, last * rows)
            terms = [dot_nn(a[at], b) for a, b in zip(left, right)]
            return functools.reduce(jnp.add, terms)

        return part_of

    def feed(normed, outs, after=()):
        everyone = links.plane_gather(normed, (1, 1))
        matrices = collect(outs)
        links.load(*after)
        gate = dot_nt(everyone, matrices[0])
        upper = dot_nt(everyone, matrices[1])
        hidden = gated_units(gate, upper).astype(BF)
        out = links.plane_scatter(eighths([hidden], [matrices[2]]), (1, 1))
        return out, (everyone, gate, upper, hidden), matrices

    vocab_ids = jnp.arange(INNER, dtype=jnp.int32)
    src_hot = (packed[0][:, None] == vocab_ids).astype(BF)
    dec_hot = (packed[1][:, None] == vocab_ids).astype(BF)
    embed_w = early[4]
    enc_zero = unproject(src_hot, embed_w)
    dec_zero = unproject(dec_hot, embed_w)
    n_zero, s_zero = norm(links.ride(enc_zero, 2), 0)
    branch, kept_enc = attention(n_zero, n_zero, early[:4], src_places, False, 2)
    enc_one = enc_zero + branch
    n_one, s_one = norm(enc_one, 1)
    branch, kept_enc_feed, feed_enc = feed(
        n_one, feed_enc, (gather_trip(own_dec[m], feed_dec[m]) for m in range(3))
    )
    enc_two = enc_one + branch
    memory, s_two = norm(enc_two, 2)
    n_three, s_three = norm(dec_zero, 3)
    branch, kept_dec = attention(n_three, n_three, weights[1], tgt_places, True, 1)
    dec_one = dec_zero + branch
    n_four, s_four = norm(dec_one, 4)
    branch, kept_cross = attention(n_four, memory, weights[2], src_places, False, 1)
    dec_two = dec_one + branch
    n_five, s_five = norm(dec_two, 5)
    branch, kept_dec_feed, feed_dec = feed(n_five, feed_dec)
    dec_three = dec_two + branch
    final, s_six = norm(dec_three, 6)

    logits = project(final, head_w)
    lse = jax.nn.logsumexp(logits, axis=-1)
    target_hot = (packed[2][:, None] == vocab_ids).astype(F32)
    picked = jnp.sum(logits * target_hot, axis=-1)
    loss_local = jnp.sum((lse - picked) * token_scale)
    grad_logits = ((jnp.exp(logits - lse[:, None]) - target_hot) * token_scale[:, None]).astype(BF)

    own_index = zc * 4 + yc * 2 + xc
    place = {"x": 1, "y": 2}
    for i, bit in enumerate(links.z_bits):
        place[bit] = 4 << i
    relative_masks = []
    for order in links.owner_orders():
        mask = [0]
        for bit in order[::-1]:
            mask = mask + [m ^ place[bit] for m in mask]
        relative_masks.append(np.repeat(np.array(mask, np.int32), width))
    columns = jnp.arange(INNER, dtype=jnp.int32)

    def shuffle_to(mask):
        moved = (mask ^ own_index) * width + columns % width
        return (columns[:, None] == moved[None, :]).astype(BF)

    to_own = shuffle_to(jnp.where(on_first, relative_masks[0], relative_masks[1]))
    to_other = shuffle_to(jnp.where(on_first, relative_masks[1], relative_masks[0]))

    def owner_grads(pairs, rides=0):
        tokens_n = max(p[0].shape[0] for p in pairs)

        def filled(value):
            return jnp.pad(value, ((0, tokens_n - value.shape[0]), (0, 0)))

        cols = jnp.concatenate([filled(p[0]) for p in pairs], 0)
        batch = (((1,), (1,)), ((0,), (0,)))

        def products(shuffle, half_of):
            moved = dot_nn(cols, shuffle).astype(BF).reshape(len(pairs), tokens_n, INNER)
            feats = jnp.stack([filled(half_of(p[1])) for p in pairs])
            return lax.dot_general(moved, feats, batch, preferred_element_type=F32).astype(BF)

        return links.owner_scatter(products(to_own, own_half), products(to_other, other_half), rides)

    def feed_back(kept, matrices, grad, outs, events=((), ()), rides=((0, 0), (0, 0))):
        everyone, gate, upper, hidden = kept
        grad_all = anchor(links.plane_gather(grad.astype(BF), rides[0]), *events[0])
        links.unload()
        _, pull = jax.vjp(gated_units, gate, upper)
        grad_gate, grad_upper = pull(dot_nt(grad_all, matrices[2]))
        gate_b, upper_b = grad_gate.astype(BF), grad_upper.astype(BF)
        grads = (
            dot_tn(gate_b, everyone).astype(BF),
            dot_tn(upper_b, everyone).astype(BF),
            dot_tn(hidden, grad_all).astype(BF),
        )
        links.load(*(scatter_trip(grads[m], outs[m]) for m in (2, 0, 1)))
        grad_normed = links.plane_scatter(eighths([gate_b, upper_b], matrices[:2]), rides[1])
        return anchor(grad_normed, *events[1])

    def attention_back(kept, normed_q, normed_kv, matrices, where, causal, grad, rides=0, events=((), ())):
        queries, kv, context = kept
        grad_b = grad.astype(BF)
        grad_context = anchor(project(grad_b, matrices[3]).astype(BF), *events[0])
        d_query, d_kv = attend_back(where, queries, grad_context, kv, causal)
        d_kv = anchor(d_kv, *events[1])
        d_kv_own = links.sequence_scatter(d_kv, rides).astype(BF)
        d_key, d_value = d_kv_own[:, :INNER], d_kv_own[:, INNER:]
        d_normed_q = unproject(d_query, matrices[0])
        d_normed_kv = unproject(d_key, matrices[1]) + unproject(d_value, matrices[2])
        pairs = [(d_query, normed_q), (d_key, normed_kv), (d_value, normed_kv), (context, grad_b)]
        return d_normed_q, d_normed_kv, pairs

    grad_final = unproject(grad_logits, head_w)
    grad_dec, gain_six = rms_reverse(dec_three, gains[6], s_six, grad_final)
    dec_feed, enc_feed = [[], [], []], [[], [], []]
    grad_normed = feed_back(kept_dec_feed, feed_dec, grad_dec, dec_feed, rides=((0, 0), (1, 1)))
    part, gain_five = rms_reverse(dec_two, gains[5], s_five, grad_normed)
    grad_dec = grad_dec + part
    d_q, grad_memory, cross_grad = attention_back(
        kept_cross, n_four, memory, weights[2], src_places, False, grad_dec, 2
    )
    cross_stages = owner_grads(cross_grad + [(grad_logits, final)])
    part, gain_four = rms_reverse(dec_one, gains[4], s_four, d_q)
    grad_dec = grad_dec + part
    d_q, d_kv, dec_grad = attention_back(
        kept_dec, n_three, n_three, weights[1], tgt_places, True, grad_dec
    )
    dec_stages = owner_grads(dec_grad)
    part, gain_three = rms_reverse(dec_zero, gains[3], s_three, d_q + d_kv)
    grad_dec = grad_dec + part
    grad_enc, gain_two = rms_reverse(enc_two, gains[2], s_two, grad_memory)
    grad_normed = feed_back(
        kept_enc_feed,
        feed_enc,
        grad_enc,
        enc_feed,
        ((cross_stages[0],), (cross_stages[1], dec_stages[0])),
        ((2, 1), (2, 1)),
    )
    dec_rows = to_rows(jnp.stack([o[0] for o in dec_feed]))
    dec_flat = flatten(dec_rows, spread, hid, period_groups)
    part, gain_one = rms_reverse(enc_one, gains[1], s_one, grad_normed)
    grad_enc = grad_enc + part
    d_q, d_kv, enc_grad = attention_back(
        kept_enc, n_zero, n_zero, weights[0], src_places, False, grad_enc, 2,
        ((cross_stages[2], dec_stages[1]), (cross_stages[3], dec_stages[2], dec_flat)),
    )
    part, gain_zero = rms_reverse(enc_zero, gains[0], s_zero, d_q + d_kv)
    grad_enc = grad_enc + part
    embed_pair = (
        jnp.concatenate([src_hot, dec_hot], 0),
        jnp.concatenate([grad_enc, grad_dec], 0).astype(BF),
    )

    early_stages = owner_grads(enc_grad + [embed_pair], 2)
    links.unload()

    def own_chunk(value):
        if rows_high > 1:
            value = value[:, :, : D // 2].reshape(value.shape[0], width, rows_high, chunk)
            value = lax.psum_scatter(value, "rh", scatter_dimension=2, tiled=True)
            value = value.reshape(value.shape[0], width, chunk)
        return value

    enc_rows = to_rows(jnp.stack([o[0] for o in enc_feed]))
    enc_flat = flatten(enc_rows, spread, hid, period_groups)
    early_red = own_chunk(early_stages[-1])
    dec_red, cross_red = own_chunk(dec_stages[-1]), own_chunk(cross_stages[-1])
    square_local = functools.reduce(
        jnp.add, [jnp.sum(v * v) for v in (early_red, dec_red, cross_red, enc_rows, dec_rows)]
    )
    lane = jnp.arange(WIDE)
    extra = jnp.where(lane == 0, square_local, 0.0) + jnp.where(lane == 1, loss_local, 0.0)
    gain_local = jnp.stack(
        [gain_zero, gain_one, gain_two, gain_three, gain_four, gain_five, gain_six, extra]
    )
    gain_local = anchor(gain_local, enc_flat, dec_flat)
    everything = links.total(gain_local, rows_high)
    loss = everything[7, 1]
    grad_norm = jnp.sqrt(everything[7, 0] + jnp.sum(everything[:7] * everything[:7]))
    count = step_count[0].astype(F32)
    scalars = jnp.stack([1.0 / (1.0 - BETA_FIRST**count), 1.0 / (1.0 - BETA_SECOND**count)])
    slot_total = tokens * cols_n

    def attn_turn(value):
        return value.transpose(0, 1, 3, 2).reshape(12, width, chunk)

    def attn_return(value):
        return value.reshape(3, 4, width, chunk).transpose(0, 1, 3, 2)

    def table_turn(value):
        return value.transpose(0, 2, 1)

    new = finish(
        (slot_total / (3.0 * INNER)) ** 0.5,
        scalars,
        everything,
        (enc_flat, dec_flat),
        (early_red, dec_red, cross_red, join_features(everything[:7])),
        tuple(v.reshape(flat_shape) for v in (feed_weights, feed_first, feed_second)),
        tuple(attn_turn(v) for v in (attn_weights, attn_first, attn_second)),
        tuple(table_turn(v) for v in (table_weights, table_first, table_second)),
        (norm_gain_stack, gain_first, gain_second),
    )
    return (
        (loss, grad_norm)
        + tuple(attn_return(v) for v in new[3:6])
        + tuple(v.reshape(feed_weights.shape) for v in new[:3])
        + tuple(table_turn(v) for v in new[6:9])
        + tuple(new[9:])
    )


def solution(mesh):
    rows_high = mesh.shape["row"] // 2
    groups = mesh.shape["col"] // 4
    split = Mesh(mesh.devices.reshape(rows_high, 2, groups, 2, 2), ("rh", "c", "z", "y", "x"))
    row, col = ("rh", "c"), ("z", "y", "x")
    attn = P(None, None, row, col)
    feed = P(None, None, col, row)
    table = P(None, row, col)
    ids = P(row, col)
    in_specs = (ids,) * 4 + (P(row),) * 3 + (P(),) + (attn,) * 3 + (feed,) * 3 + (table,) * 3 + (P(),) * 3
    out_specs = (P(), P()) + (attn,) * 3 + (feed,) * 3 + (table,) * 3 + (P(),) * 3
    return jax.shard_map(
        functools.partial(step, (rows_high, groups)),
        mesh=split,
        in_specs=in_specs,
        out_specs=out_specs,
        check_vma=False,
    )
```

```python
import functools

import jax
import jax.numpy as jnp
import numpy as np
from jax import lax
from jax.experimental import pallas as pl
from jax.experimental.pallas import tpu as pltpu
from jax.sharding import Mesh, PartitionSpec as P

D = 1472
HEADS = 6
HEAD_DIM = 64
NLANG = 4
INNER = 384
FF = 3584
LANES = 128
HALF = 768
WIDE = 2 * HALF

RMS_EPS = 1e-06
CLIP_NORM = 0.01
BETA_FIRST = 0.9
BETA_SECOND = 0.999
ADAM_EPS = 1e-08
MATRIX_RATE = 0.05
GAIN_RATE = 0.2
DECAY_STEP = 0.005
MASKED = -1000000000.0
PERIOD = 896
KEYS = 256
MIB = 1024 * 1024
BF = jnp.bfloat16
F32 = jnp.float32


def dot_nn(a, b):
    return lax.dot_general(a, b, (((1,), (0,)), ((), ())), preferred_element_type=F32)


def dot_nt(a, b):
    return lax.dot_general(a, b, (((1,), (1,)), ((), ())), preferred_element_type=F32)


def dot_tn(a, b):
    return lax.dot_general(a, b, (((0,), (0,)), ((), ())), preferred_element_type=F32)


def flat_pieces(hid):
    found = []
    for t in range(PERIOD // LANES):
        at = LANES * t
        while at < LANES * (t + 1):
            j = at // hid
            end = min(LANES * (t + 1), (j + 1) * hid)
            found.append((t, at - LANES * t, j, at - j * hid, end - at))
            at = end
    return found


def unflatten_kernel(hid, groups, flat_ref, spread_ref, out_ref, acc_ref):
    chunks = PERIOD // LANES
    acc_ref[...] = jnp.zeros_like(acc_ref)
    for t in range(chunks):
        rows = flat_ref[0, pl.ds(t, groups, stride=chunks), :].astype(BF)
        for piece_t, lane, j, first, length in flat_pieces(hid):
            if piece_t == t:
                placed = dot_tn(rows, spread_ref[j])
                acc_ref[first : first + length, :] += placed[lane : lane + length, :]
    out_ref[0] = acc_ref[...].astype(BF)


def unflatten(flat, spread, hid, groups):
    count, flat_rows, _ = flat.shape
    lanes = spread.shape[2]
    return pl.pallas_call(
        functools.partial(unflatten_kernel, hid, groups),
        out_shape=jax.ShapeDtypeStruct((count, hid, lanes), BF),
        grid=(count,),
        in_specs=[
            pl.BlockSpec((1, flat_rows, LANES), lambda i: (i, 0, 0)),
            pl.BlockSpec(spread.shape, lambda i: (0, 0, 0)),
        ],
        out_specs=pl.BlockSpec((1, hid, lanes), lambda i: (i, 0, 0)),
        scratch_shapes=[pltpu.VMEM((hid, lanes), F32)],
        compiler_params=pltpu.CompilerParams(vmem_limit_bytes=10 * MIB),
        name="unflatten",
    )(flat, spread)


def flatten_kernel(hid, groups, grad_ref, spread_ref, out_ref):
    chunks = PERIOD // LANES
    grads = grad_ref[0].astype(BF)
    for t in range(chunks):
        total = jnp.zeros((groups, LANES), F32)
        for piece_t, lane, j, first, length in flat_pieces(hid):
            if piece_t == t:
                rows = grads[first : first + length, :]
                parts = []
                if lane > 0:
                    parts.append(jnp.zeros((lane, rows.shape[1]), BF))
                parts.append(rows)
                if lane + length < LANES:
                    parts.append(jnp.zeros((LANES - lane - length, rows.shape[1]), BF))
                rows = jnp.concatenate(parts, 0) if len(parts) > 1 else rows
                total = total + dot_nt(spread_ref[j], rows)
        out_ref[0, pl.ds(t, groups, stride=chunks), :] = total


def flatten(grads, spread, hid, groups):
    count, _, lanes = grads.shape
    flat_rows = groups * PERIOD // LANES
    return pl.pallas_call(
        functools.partial(flatten_kernel, hid, groups),
        out_shape=jax.ShapeDtypeStruct((count, flat_rows, LANES), F32),
        grid=(count,),
        in_specs=[
            pl.BlockSpec((1, hid, lanes), lambda i: (i, 0, 0)),
            pl.BlockSpec(spread.shape, lambda i: (0, 0, 0)),
        ],
        out_specs=pl.BlockSpec((1, flat_rows, LANES), lambda i: (i, 0, 0)),
        compiler_params=pltpu.CompilerParams(vmem_limit_bytes=10 * MIB),
        name="flatten",
    )(grads, spread)


def finish_kernel(
    slot_rate, scal_ref, all_ref, enc_ref, dec_ref, early_ref, own_ref, cross_ref, gain_ref,
    fw_ref, fm_ref, fv_ref, aw_ref, am_ref, av_ref, tw_ref, tm_ref, tv_ref, gw_ref, gm_ref, gv_ref,
    fm_out, fv_out, fw_out, am_out, av_out, aw_out, tm_out, tv_out, tw_out, gm_out, gv_out, gw_out,
):
    at = pl.program_id(0)
    gains = all_ref[0:7, :]
    square = jnp.sum(jnp.sum(gains * gains, axis=1, keepdims=True), axis=0, keepdims=True)
    norm = jnp.sqrt(all_ref[7:8, 0:1] + square)
    clip = CLIP_NORM / jnp.maximum(norm, CLIP_NORM)
    scales = (clip, scal_ref[0], scal_ref[1])

    def feed(grad_ref):
        fm_out[0], fv_out[0], fw_out[0] = adam_rule(
            fw_ref[0], fm_ref[0], fv_ref[0], grad_ref[0], *scales, MATRIX_RATE, DECAY_STEP
        )

    @pl.when(at < 3)
    def _():
        feed(enc_ref)

    @pl.when(at >= 3)
    def _():
        feed(dec_ref)

    chunk = aw_ref.shape[2]
    grads = [ref.at[i] for ref in (early_ref, own_ref, cross_ref) for i in range(4)]
    for i, grad in enumerate(grads):

        @pl.when(at == i // 2)
        def _(i=i, grad=grad):
            rate = slot_rate if i % 4 == 3 else MATRIX_RATE
            k = i % 2
            am_out[k], av_out[k], aw_out[k] = adam_rule(
                aw_ref[k], am_ref[k], av_ref[k], grad[:, :chunk], *scales, rate, DECAY_STEP
            )

    @pl.when(at == 5)
    def _():
        for i, (grad, rate) in enumerate(((early_ref.at[4], 1.0), (cross_ref.at[4], 1.5 * D ** (-0.5)))):
            tm_out[i], tv_out[i], tw_out[i] = adam_rule(
                tw_ref[i], tm_ref[i], tv_ref[i], grad[:, :chunk], *scales, rate, DECAY_STEP
            )
        gm_out[...], gv_out[...], gw_out[...] = adam_rule(
            gw_ref[...], gm_ref[...], gv_ref[...], gain_ref[...], *scales, GAIN_RATE, 0.0
        )


def finish(slot_rate, scalars, everything, feed_grads, rest_grads, feed, attn, table, gain):
    block = (1,) + feed[0].shape[1:]
    flat = pl.BlockSpec(block, lambda i: (i, 0, 0))

    def whole(value):
        return pl.BlockSpec(value.shape, lambda i: (0,) * value.ndim)

    def like(value):
        return jax.ShapeDtypeStruct(value.shape, F32)

    rest = table + gain
    pair = pl.BlockSpec((2,) + attn[0].shape[1:], lambda i: (i, 0, 0))
    return pl.pallas_call(
        functools.partial(finish_kernel, slot_rate),
        out_shape=[like(v) for v in feed + attn + rest],
        grid=(6,),
        in_specs=[pl.BlockSpec(memory_space=pltpu.SMEM), whole(everything)]
        + [
            pl.BlockSpec(block, lambda i: (jnp.minimum(i, 2), 0, 0)),
            pl.BlockSpec(block, lambda i: (jnp.maximum(i - 3, 0), 0, 0)),
        ]
        + [whole(v) for v in rest_grads]
        + [flat] * 3
        + [pair] * 3
        + [whole(v) for v in rest],
        out_specs=[flat] * 3 + [pair] * 3 + [whole(v) for v in rest],
        compiler_params=pltpu.CompilerParams(vmem_limit_bytes=56 * MIB),
        name="finish",
    )(scalars, everything, *feed_grads, *rest_grads, *feed, *attn, *rest)


def head_lanes(shape, h):
    lane = lax.broadcasted_iota(jnp.int32, shape, 1)
    return (lane < HEAD_DIM) if h == 0 else (lane >= HEAD_DIM)


def attend_kernel(causal, where_ref, q_ref, kv_ref, out_ref, pos_ref):
    count = q_ref.shape[0]
    length = kv_ref.shape[0]
    blocks = length // count
    limit = where_ref[blocks]
    first = where_ref[blocks + 1]
    for b in range(blocks):
        pos_ref[:, b * count : (b + 1) * count] = (
            lax.broadcasted_iota(jnp.int32, (8, count), 1) + where_ref[b]
        )
    pos = pos_ref[0:1, :]
    last = jnp.full((count, 1), limit - 1, jnp.int32)
    if causal:
        last = jnp.minimum(last, first + lax.broadcasted_iota(jnp.int32, (count, 1), 0))
    allowed = pos <= last
    for p in range(3):
        lanes = slice(p * LANES, (p + 1) * LANES)
        values = slice(INNER + p * LANES, INNER + (p + 1) * LANES)
        queries = q_ref[:, lanes] * HEAD_DIM ** (-0.5)
        context = []
        for h in range(2):
            own = jnp.where(head_lanes(queries.shape, h), queries, jnp.zeros_like(queries))
            scores = dot_nt(own, kv_ref[:, lanes])
            scores = jnp.where(allowed, scores, MASKED)
            raised = jnp.exp(scores - jnp.max(scores, axis=1, keepdims=True))
            probs = raised * (1.0 / jnp.sum(raised, axis=1, keepdims=True))
            context.append(dot_nn(probs.astype(BF), kv_ref[:, values]))
        out_ref[:, lanes] = jnp.where(
            head_lanes(context[0].shape, 0), context[0], context[1]
        ).astype(BF)


def attend(where, queries, kv, causal):
    count = queries.shape[0]
    length = kv.shape[0]
    vmem = pl.BlockSpec(memory_space=pltpu.VMEM)
    return pl.pallas_call(
        functools.partial(attend_kernel, causal),
        out_shape=jax.ShapeDtypeStruct((count, INNER), BF),
        in_specs=[pl.BlockSpec(memory_space=pltpu.SMEM)] + [vmem] * 2,
        out_specs=vmem,
        scratch_shapes=[pltpu.VMEM((8, length), jnp.int32)],
        compiler_params=pltpu.CompilerParams(vmem_limit_bytes=8 * MIB + 4096 * length),
        cost_estimate=pl.CostEstimate(
            flops=4 * count * length * INNER * 2,
            transcendentals=HEADS * count * length,
            bytes_accessed=4 * length * INNER,
        ),
        name="attend",
    )(where, queries, kv)


def attend_back_kernel(causal, where_ref, q_ref, g_ref, kv_ref, dq_ref, dkv_ref, pos_ref, s_ref, dp_ref):
    count = q_ref.shape[0]
    length = kv_ref.shape[0]
    blocks = length // count
    limit = where_ref[blocks]
    first = where_ref[blocks + 1]
    scale = HEAD_DIM ** (-0.5)
    last = jnp.full((1, count), limit - 1, jnp.int32)
    if causal:
        last = jnp.minimum(last, first + lax.broadcasted_iota(jnp.int32, (1, count), 1))
    for b in range(blocks):
        pos_ref[b * count : (b + 1) * count, :] = (
            lax.broadcasted_iota(jnp.int32, (count, count), 0) + where_ref[b]
        )
    for p in range(3):
        lanes = slice(p * LANES, (p + 1) * LANES)
        values = slice(INNER + p * LANES, INNER + (p + 1) * LANES)
        queries = q_ref[:, lanes] * scale
        grads = g_ref[:, lanes]
        d_query = []
        for h in range(2):
            own_q = jnp.where(head_lanes(queries.shape, h), queries, jnp.zeros_like(queries))
            own_g = jnp.where(head_lanes(grads.shape, h), grads, jnp.zeros_like(grads))

            def rows(i):
                return pl.ds(pl.multiple_of(i * KEYS, KEYS), KEYS)

            def score_pass(i, peak):
                at = rows(i)
                scores = dot_nt(kv_ref[at, lanes], own_q)
                scores = jnp.where(pos_ref[at, :] <= last, scores, MASKED)
                s_ref[at, :] = scores
                return jnp.maximum(peak, jnp.max(scores, axis=0, keepdims=True))

            def sum_pass(i, sums):
                at = rows(i)
                raised = jnp.exp(s_ref[at, :] - peak)
                d_probs = dot_nt(kv_ref[at, values], own_g)
                s_ref[at, :] = raised
                dp_ref[at, :] = d_probs
                return (
                    sums[0] + jnp.sum(raised, axis=0, keepdims=True),
                    sums[1] + jnp.sum(raised * d_probs, axis=0, keepdims=True),
                )

            def grad_pass(i, total):
                at = rows(i)
                probs = s_ref[at, :] * share
                d_scores = (probs * (dp_ref[at, :] - inner)).astype(BF)
                key_part = dot_nn(d_scores, own_q).astype(BF)
                value_part = dot_nn(probs.astype(BF), own_g).astype(BF)
                dkv_ref[at, lanes] = key_part if h == 0 else dkv_ref[at, lanes] + key_part
                dkv_ref[at, values] = value_part if h == 0 else dkv_ref[at, values] + value_part
                return total + dot_tn(d_scores, kv_ref[at, lanes])

            steps = length // KEYS
            none = jnp.zeros((1, count), F32)
            peak = lax.fori_loop(0, steps, score_pass, none + MASKED, unroll=True)
            total, weighted = lax.fori_loop(0, steps, sum_pass, (none, none), unroll=True)
            share = 1.0 / total
            inner = weighted * share
            d_query.append(
                lax.fori_loop(0, steps, grad_pass, jnp.zeros((count, LANES), F32), unroll=True) * scale
            )
        dq_ref[:, lanes] = jnp.where(
            head_lanes(d_query[0].shape, 0), d_query[0], d_query[1]
        ).astype(BF)


def attend_back(where, queries, grads, kv, causal):
    count = queries.shape[0]
    length = kv.shape[0]
    vmem = pl.BlockSpec(memory_space=pltpu.VMEM)
    return pl.pallas_call(
        functools.partial(attend_back_kernel, causal),
        out_shape=(
            jax.ShapeDtypeStruct((count, INNER), BF),
            jax.ShapeDtypeStruct((length, 2 * INNER), BF),
        ),
        in_specs=[pl.BlockSpec(memory_space=pltpu.SMEM)] + [vmem] * 3,
        out_specs=(vmem,) * 2,
        scratch_shapes=[
            pltpu.VMEM((length, count), jnp.int32),
            pltpu.VMEM((length, count), F32),
            pltpu.VMEM((length, count), F32),
        ],
        compiler_params=pltpu.CompilerParams(vmem_limit_bytes=8 * MIB + 8192 * length),
        cost_estimate=pl.CostEstimate(
            flops=10 * count * length * INNER * 2,
            transcendentals=HEADS * count * length,
            bytes_accessed=8 * length * INNER,
        ),
        name="attend_back",
    )(where, queries, grads, kv)


def rms_scale(stream):
    return lax.rsqrt(jnp.sum(stream * stream, axis=-1, keepdims=True) * (1.0 / D) + RMS_EPS)


def rms_reverse(stream, gain, scale, grad_out):
    weighted = grad_out * gain
    inner_mean = jnp.sum(weighted * stream, axis=-1, keepdims=True) * (1.0 / D)
    grad_in = scale * weighted - stream * (scale * scale * scale) * inner_mean
    grad_gain = jnp.sum(grad_out * stream * scale, axis=0)
    return (grad_in, grad_gain)


def gated_units(gate, upper):
    return jax.nn.gelu(gate, approximate=True) * upper


def adam_rule(weight, first, second, grad, clip, first_scale, second_scale, rate, decay_step):
    clipped = grad * clip
    first_new = BETA_FIRST * first + (1.0 - BETA_FIRST) * clipped
    second_new = BETA_SECOND * second + (1.0 - BETA_SECOND) * clipped * clipped
    ratio = first_new * first_scale / (jnp.sqrt(second_new * second_scale) + ADAM_EPS)
    return (first_new, second_new, weight - rate * ratio - decay_step * weight)


def anchor(value, *events):
    return lax.optimization_barrier((value,) + events)[0] if events else value


class Links:
    def __init__(self, groups):
        self.groups = groups
        self.z_bits = [f"z{i}" for i in range(groups.bit_length() - 1)]
        self.near = self.z_bits[:-1] if len(self.z_bits) > 1 else []
        self.cargo = []

    def load(self, *trips):
        self.cargo += [(trip, next(trip)) for trip in trips]

    def ship(self):
        trip, (value, step) = self.cargo.pop(0)
        return trip, self.ring(value, step)

    def land(self, trip, came):
        try:
            self.cargo.insert(min(1, len(self.cargo)), (trip, trip.send(came)))
        except StopIteration:
            pass

    def ride(self, value, count=1):
        sent = [self.ship() for _ in range(min(count, len(self.cargo)))]
        if sent:
            came = lax.optimization_barrier((value,) + tuple(c for _, c in sent))
            value = came[0]
            for (trip, _), c in zip(sent, came[1:]):
                self.land(trip, c)
        return value

    def unload(self):
        while self.cargo:
            self.land(*self.ship())

    def swap(self, value, bit):
        if bit[0] == "z":
            step = 1 << int(bit[1:])
            return lax.ppermute(value, "z", [(i, i ^ step) for i in range(self.groups)])
        return lax.ppermute(value, bit, [(0, 1), (1, 0)])

    def swap_by_core(self, value, bits):
        chips = 4 * self.groups
        masks = {"x": 1, "y": 2}
        for i, bit in enumerate(self.z_bits):
            masks[bit] = 4 << i
        pairs = [(c * chips + k, c * chips + (k ^ masks[bits[c]])) for c in range(2) for k in range(chips)]
        return lax.ppermute(value, ("c", "z", "y", "x"), pairs)

    def ring(self, value, step):
        n = self.groups
        return lax.ppermute(value, "z", [(i, (i + step) % n) for i in range(n)])

    def plane_gather(self, own, rides=(0, 0)):
        first = self.ride(self.swap_by_core(own, "xy"), rides[0])
        pair = jnp.concatenate([own, first], 0)
        second = self.ride(self.swap_by_core(pair, "yx"), rides[1])
        mine = jnp.concatenate([pair, second], 0)
        return jnp.concatenate([mine, self.swap(mine, "c")], 0)

    def plane_scatter(self, part_of, rides=(0, 0)):
        total = self.swap(part_of(4, 8).astype(BF), "c").astype(F32) + part_of(0, 4)
        rows = total.shape[0] // 4
        far = self.ride(self.swap_by_core(total[2 * rows :].astype(BF), "yx"), rides[0]).astype(F32)
        near = (total[rows : 2 * rows] + far[rows:]).astype(BF)
        near = self.ride(self.swap_by_core(near, "xy"), rides[1]).astype(F32)
        return total[:rows] + far[:rows] + near

    def orders(self):
        return [self.near + ["x", "y"], self.near + ["y", "x"]]

    def sequence_gather(self, part, rides=0):
        for bits in zip(*self.orders()):
            came = self.swap_by_core(part, bits)
            if bits[0][0] != "z":
                came = self.ride(came, rides)
            part = jnp.concatenate([part, came], 0)
        return jnp.concatenate([part, self.swap(part, "c")], 0)

    def sequence_scatter(self, part, rides=0):
        rows = part.shape[0] // 2
        part = part[:rows].astype(F32) + self.swap(part[rows:], "c").astype(F32)
        for bits in list(zip(*self.orders()))[::-1]:
            rows = part.shape[0] // 2
            came = self.swap_by_core(part[rows:].astype(BF), bits)
            if bits[0][0] != "z":
                came = self.ride(came, rides)
            part = part[:rows] + came.astype(F32)
        return part

    def owner_orders(self):
        return [["x", "y"] + self.z_bits, ["y", "x"] + self.z_bits]

    def owner_scatter(self, keep, send, rides=0):
        part = keep.astype(F32) + self.swap(send, "c").astype(F32)
        stages = [part]
        for bits in zip(*self.owner_orders()):
            rows = part.shape[1] // 2
            came = self.swap_by_core(part[:, rows:].astype(BF), bits)
            if bits[0][0] != "z":
                came = self.ride(came, rides)
            part = part[:, :rows] + came.astype(F32)
            stages.append(part)
        return stages

    def total(self, value, rows_high):
        for bit in ["c", "x", "y"] + self.z_bits:
            value = value + self.swap(value, bit)
        return lax.psum(value, "rh") if rows_high > 1 else value


def step(
    shape,
    source_bytes,
    decoder_bytes,
    target_bytes,
    target_keep,
    source_length,
    target_length,
    language,
    step_count,
    attn_weights,
    attn_first,
    attn_second,
    feed_weights,
    feed_first,
    feed_second,
    table_weights,
    table_first,
    table_second,
    norm_gain_stack,
    gain_first,
    gain_second,
):
    rows_high, groups = shape
    rows_n, cols_n = 2 * rows_high, 4 * groups
    links = Links(groups)
    core, zc, yc, xc = (lax.axis_index(a) for a in ("c", "z", "y", "x"))
    on_first = core == 0
    tokens = source_bytes.shape[1]
    chunk = attn_weights.shape[2]
    width = attn_weights.shape[3]
    everywhere = ("rh", "c", "z", "y", "x")

    def own_half(value):
        return jnp.where(on_first, value[..., :HALF], value[..., HALF:])

    def other_half(value):
        return jnp.where(on_first, value[..., HALF:], value[..., :HALF])

    def in_order(own, other, axis):
        return jnp.concatenate(
            [jnp.where(on_first, own, other), jnp.where(on_first, other, own)], axis
        )

    def widen(value):
        pad = [(0, 0)] * (value.ndim - 1) + [(0, HALF - value.shape[-1])]
        return jnp.pad(value, pad)

    def spread_features(value):
        split = value.reshape(value.shape[0], rows_high, 2, chunk).transpose(0, 2, 1, 3)
        return widen(split.reshape(value.shape[0], 2, D // 2)).reshape(value.shape[0], WIDE)

    def join_features(value):
        if rows_high == 1:
            return jnp.concatenate([value[:, : D // 2], value[:, HALF : HALF + D // 2]], 1)
        split = value.reshape(value.shape[0], 2, HALF)[:, :, : D // 2]
        split = split.reshape(value.shape[0], 2, rows_high, chunk).transpose(0, 2, 1, 3)
        return split.reshape(value.shape[0], D)

    half = groups // 2
    packed = jnp.concatenate(
        [source_bytes, decoder_bytes, target_bytes, target_keep]
        + [
            jnp.broadcast_to(v[:, None], (1, tokens))
            for v in (source_length, target_length, language, language)
        ],
        0,
    )
    pairs = []
    for c in range(2):
        for k in range(cols_n):
            block = (((k // 4) % half) * 4 + k % 4) * 2 + c
            pairs.append(((k // 4 // half) * cols_n + block, c * cols_n + k))
    packed = lax.ppermute(packed, ("c", "z", "y", "x"), pairs)
    block = (((zc % half) * 2 + yc) * 2 + xc) * 2 + core
    first_pos = block * tokens
    src_limit, tgt_limit, tongue = packed[4, 0], packed[5, 0], packed[6, 0]
    positions = first_pos + jnp.arange(tokens, dtype=jnp.int32)
    weight = ((positions < tgt_limit) & (packed[3] > 0)).astype(F32)
    member = (tongue == jnp.arange(LANES, dtype=jnp.int32)).astype(F32)
    bit_value = {"c": 1, "x": 2, "y": 4}
    for i, bit in enumerate(links.near):
        bit_value[bit] = 8 << i
    masks = []
    for order in links.orders():
        mask = [0]
        for bit in order:
            mask = mask + [m ^ bit_value[bit] for m in mask]
        masks.append(mask)
    masks = np.array([masks[c] + [m ^ 1 for m in masks[1 - c]] for c in range(2)], np.int32)
    firsts = (jnp.where(on_first, masks[0], masks[1]) ^ block) * tokens

    def places(limit):
        return jnp.concatenate([firsts, jnp.stack([limit, first_pos]).astype(jnp.int32)])

    src_places, tgt_places = places(src_limit), places(tgt_limit)

    attn_t = attn_weights.transpose(0, 1, 3, 2)
    table_t = table_weights.transpose(0, 2, 1)

    def gather_tiles(tiles):
        tiles = tiles.astype(BF)
        if rows_high == 1 and tiles.shape[2] < HALF:
            tiles = widen(tiles)
        full = lax.all_gather(tiles[:, None], everywhere, axis=1, tiled=True)
        if rows_high == 1:
            return full.reshape(tiles.shape[0], 2, INNER, HALF)
        full = full.reshape(tiles.shape[0], rows_high, 2, INNER, chunk).transpose(0, 2, 3, 1, 4)
        return widen(full.reshape(tiles.shape[0], 2, INNER, D // 2))

    early_tiles = jnp.concatenate([attn_t[0], table_t[:1]], 0)
    own_counts = (member * jnp.sum(weight))[: HALF - D // 2]
    if rows_high == 1:
        lane_row = jnp.pad(own_counts, (D // 2, 0))[None, None]
        place = lax.broadcasted_iota(jnp.int32, (5, width, 1), 0) + lax.broadcasted_iota(jnp.int32, (5, width, 1), 1)
        early = gather_tiles(widen(early_tiles) + jnp.where(place == 0, lane_row, 0.0))
        counts = jnp.sum(early[0, :, ::width, D // 2 :].astype(F32), axis=(0, 1))
    else:
        early = gather_tiles(early_tiles)
        counts = lax.psum(own_counts, everywhere)
    inverse = 1.0 / (NLANG * jnp.maximum(counts, 1.0))
    token_scale = weight * jnp.sum(member[: HALF - D // 2] * inverse)

    def project(value, matrix):
        return dot_nt(value[:, :HALF], matrix[0]) + dot_nt(value[:, HALF:], matrix[1])

    def unproject(value, matrix):
        return jnp.concatenate([dot_nn(value, matrix[0]), dot_nn(value, matrix[1])], 1)

    hid = FF // cols_n
    hid_half = hid // 2
    period_rows = PERIOD // hid
    period_groups = chunk // period_rows
    lanes_own = HALF if rows_high == 1 else chunk
    shape3 = (period_rows, period_groups, lanes_own)
    spread = (
        lax.broadcasted_iota(jnp.int32, shape3, 2)
        == lax.broadcasted_iota(jnp.int32, shape3, 1) * period_rows
        + lax.broadcasted_iota(jnp.int32, shape3, 0)
    ).astype(BF)
    flat_shape = (6, chunk * hid // LANES, LANES)
    feed_t = unflatten(feed_weights.reshape(flat_shape), spread, hid, period_groups)
    if rows_high > 1:
        feed_t = lax.all_gather(feed_t[None], "rh", axis=0, tiled=True)
        feed_t = widen(feed_t.transpose(1, 2, 0, 3).reshape(6, hid, D // 2))

    def halves_joined(mine):
        keep = jnp.where(on_first, mine[:, :hid_half], mine[:, hid_half:])
        send = jnp.where(on_first, mine[:, hid_half:], mine[:, :hid_half])
        return in_order(keep, links.swap(send, "c"), 2)

    def gather_trip(own, out):
        held = [own]
        for _ in range(groups - 1):
            held.append((yield held[-1], 1))
        out.append(jnp.concatenate(held, 0))

    def scatter_trip(grads, out):
        grads = grads.reshape(groups, hid_half, WIDE)
        value = grads[groups - 1]
        for s in range(groups - 2, -1, -1):
            came = yield value.astype(BF), -1
            value = grads[s].astype(F32) + came.astype(F32)
        out.append(value)

    def collect(outs):
        links.unload()
        return [o[0] for o in outs]

    def to_rows(value):
        keep, send = own_half(value).astype(F32), other_half(value).astype(BF)
        full = in_order(keep, links.swap(send, "c").astype(F32), 1)
        if rows_high > 1:
            full = full[:, :, : D // 2].reshape(3, hid, rows_high, chunk)
            full = lax.psum_scatter(full, "rh", scatter_dimension=2, tiled=True)
            full = full.reshape(3, hid, chunk)
        return full

    late = gather_tiles(jnp.concatenate([attn_t[1], attn_t[2], table_t[1:]], 0))
    weights = [early[:4], late[:4], late[4:8]]
    head_w = late[8]
    own_enc, own_dec = halves_joined(feed_t[:3]), halves_joined(feed_t[3:])
    feed_enc, feed_dec = [[], [], []], [[], [], []]
    links.load(*(gather_trip(own_enc[m], feed_enc[m]) for m in range(3)))
    gains = spread_features(norm_gain_stack)

    def norm(stream, index):
        scale = rms_scale(stream)
        return (stream * scale * gains[index]).astype(BF), scale

    def attention(normed_q, normed_kv, matrices, where, causal, rides):
        queries = project(normed_q, matrices[0]).astype(BF)
        kv = jnp.concatenate([project(normed_kv, matrices[1]), project(normed_kv, matrices[2])], 1)
        kv = links.sequence_gather(kv.astype(BF), rides)
        context = attend(where, queries, kv, causal)
        return unproject(context, matrices[3]), (queries, kv, context)

    def eighths(left, right):
        rows = left[0].shape[0] // 8

        def part_of(first, last):
            at = slice(first * rows, last * rows)
            terms = [dot_nn(a[at], b) for a, b in zip(left, right)]
            return functools.reduce(jnp.add, terms)

        return part_of

    def feed(normed, outs, after=()):
        everyone = links.plane_gather(normed, (1, 1))
        matrices = collect(outs)
        links.load(*after)
        gate = dot_nt(everyone, matrices[0])
        upper = dot_nt(everyone, matrices[1])
        hidden = gated_units(gate, upper).astype(BF)
        out = links.plane_scatter(eighths([hidden], [matrices[2]]), (1, 1))
        return out, (everyone, gate, upper, hidden), matrices

    vocab_ids = jnp.arange(INNER, dtype=jnp.int32)
    src_hot = (packed[0][:, None] == vocab_ids).astype(BF)
    dec_hot = (packed[1][:, None] == vocab_ids).astype(BF)
    embed_w = early[4]
    enc_zero = unproject(src_hot, embed_w)
    dec_zero = unproject(dec_hot, embed_w)
    n_zero, s_zero = norm(links.ride(enc_zero, 2), 0)
    branch, kept_enc = attention(n_zero, n_zero, early[:4], src_places, False, 2)
    enc_one = enc_zero + branch
    n_one, s_one = norm(enc_one, 1)
    branch, kept_enc_feed, feed_enc = feed(
        n_one, feed_enc, (gather_trip(own_dec[m], feed_dec[m]) for m in range(3))
    )
    enc_two = enc_one + branch
    memory, s_two = norm(enc_two, 2)
    n_three, s_three = norm(dec_zero, 3)
    branch, kept_dec = attention(n_three, n_three, weights[1], tgt_places, True, 1)
    dec_one = dec_zero + branch
    n_four, s_four = norm(dec_one, 4)
    branch, kept_cross = attention(n_four, memory, weights[2], src_places, False, 1)
    dec_two = dec_one + branch
    n_five, s_five = norm(dec_two, 5)
    branch, kept_dec_feed, feed_dec = feed(n_five, feed_dec)
    dec_three = dec_two + branch
    final, s_six = norm(dec_three, 6)

    logits = project(final, head_w)
    lse = jax.nn.logsumexp(logits, axis=-1)
    target_hot = (packed[2][:, None] == vocab_ids).astype(F32)
    picked = jnp.sum(logits * target_hot, axis=-1)
    loss_local = jnp.sum((lse - picked) * token_scale)
    grad_logits = ((jnp.exp(logits - lse[:, None]) - target_hot) * token_scale[:, None]).astype(BF)

    own_index = zc * 4 + yc * 2 + xc
    place = {"x": 1, "y": 2}
    for i, bit in enumerate(links.z_bits):
        place[bit] = 4 << i
    relative_masks = []
    for order in links.owner_orders():
        mask = [0]
        for bit in order[::-1]:
            mask = mask + [m ^ place[bit] for m in mask]
        relative_masks.append(np.repeat(np.array(mask, np.int32), width))
    columns = jnp.arange(INNER, dtype=jnp.int32)

    def shuffle_to(mask):
        moved = (mask ^ own_index) * width + columns % width
        return (columns[:, None] == moved[None, :]).astype(BF)

    to_own = shuffle_to(jnp.where(on_first, relative_masks[0], relative_masks[1]))
    to_other = shuffle_to(jnp.where(on_first, relative_masks[1], relative_masks[0]))

    def owner_grads(pairs, rides=0):
        tokens_n = max(p[0].shape[0] for p in pairs)

        def filled(value):
            return jnp.pad(value, ((0, tokens_n - value.shape[0]), (0, 0)))

        cols = jnp.concatenate([filled(p[0]) for p in pairs], 0)
        batch = (((1,), (1,)), ((0,), (0,)))

        def products(shuffle, half_of):
            moved = dot_nn(cols, shuffle).astype(BF).reshape(len(pairs), tokens_n, INNER)
            feats = jnp.stack([filled(half_of(p[1])) for p in pairs])
            return lax.dot_general(moved, feats, batch, preferred_element_type=F32).astype(BF)

        return links.owner_scatter(products(to_own, own_half), products(to_other, other_half), rides)

    def feed_back(kept, matrices, grad, outs, events=((), ()), rides=((0, 0), (0, 0))):
        everyone, gate, upper, hidden = kept
        grad_all = anchor(links.plane_gather(grad.astype(BF), rides[0]), *events[0])
        links.unload()
        _, pull = jax.vjp(gated_units, gate, upper)
        grad_gate, grad_upper = pull(dot_nt(grad_all, matrices[2]))
        gate_b, upper_b = grad_gate.astype(BF), grad_upper.astype(BF)
        grads = (
            dot_tn(gate_b, everyone).astype(BF),
            dot_tn(upper_b, everyone).astype(BF),
            dot_tn(hidden, grad_all).astype(BF),
        )
        links.load(*(scatter_trip(grads[m], outs[m]) for m in (2, 0, 1)))
        grad_normed = links.plane_scatter(eighths([gate_b, upper_b], matrices[:2]), rides[1])
        return anchor(grad_normed, *events[1])

    def attention_back(kept, normed_q, normed_kv, matrices, where, causal, grad, rides=0, events=((), ())):
        queries, kv, context = kept
        grad_b = grad.astype(BF)
        grad_context = anchor(project(grad_b, matrices[3]).astype(BF), *events[0])
        d_query, d_kv = attend_back(where, queries, grad_context, kv, causal)
        d_kv = anchor(d_kv, *events[1])
        d_kv_own = links.sequence_scatter(d_kv, rides).astype(BF)
        d_key, d_value = d_kv_own[:, :INNER], d_kv_own[:, INNER:]
        d_normed_q = unproject(d_query, matrices[0])
        d_normed_kv = unproject(d_key, matrices[1]) + unproject(d_value, matrices[2])
        pairs = [(d_query, normed_q), (d_key, normed_kv), (d_value, normed_kv), (context, grad_b)]
        return d_normed_q, d_normed_kv, pairs

    grad_final = unproject(grad_logits, head_w)
    grad_dec, gain_six = rms_reverse(dec_three, gains[6], s_six, grad_final)
    dec_feed, enc_feed = [[], [], []], [[], [], []]
    grad_normed = feed_back(kept_dec_feed, feed_dec, grad_dec, dec_feed, rides=((0, 0), (1, 1)))
    part, gain_five = rms_reverse(dec_two, gains[5], s_five, grad_normed)
    grad_dec = grad_dec + part
    d_q, grad_memory, cross_grad = attention_back(
        kept_cross, n_four, memory, weights[2], src_places, False, grad_dec, 2
    )
    cross_stages = owner_grads(cross_grad + [(grad_logits, final)])
    part, gain_four = rms_reverse(dec_one, gains[4], s_four, d_q)
    grad_dec = grad_dec + part
    d_q, d_kv, dec_grad = attention_back(
        kept_dec, n_three, n_three, weights[1], tgt_places, True, grad_dec
    )
    dec_stages = owner_grads(dec_grad)
    part, gain_three = rms_reverse(dec_zero, gains[3], s_three, d_q + d_kv)
    grad_dec = grad_dec + part
    grad_enc, gain_two = rms_reverse(enc_two, gains[2], s_two, grad_memory)
    grad_normed = feed_back(
        kept_enc_feed,
        feed_enc,
        grad_enc,
        enc_feed,
        ((cross_stages[0],), (cross_stages[1], dec_stages[0])),
        ((2, 1), (2, 1)),
    )
    dec_rows = to_rows(jnp.stack([o[0] for o in dec_feed]))
    dec_flat = flatten(dec_rows, spread, hid, period_groups)
    part, gain_one = rms_reverse(enc_one, gains[1], s_one, grad_normed)
    grad_enc = grad_enc + part
    d_q, d_kv, enc_grad = attention_back(
        kept_enc, n_zero, n_zero, weights[0], src_places, False, grad_enc, 2,
        ((cross_stages[2], dec_stages[1]), (cross_stages[3], dec_stages[2], dec_flat)),
    )
    part, gain_zero = rms_reverse(enc_zero, gains[0], s_zero, d_q + d_kv)
    grad_enc = grad_enc + part
    embed_pair = (
        jnp.concatenate([src_hot, dec_hot], 0),
        jnp.concatenate([grad_enc, grad_dec], 0).astype(BF),
    )

    early_stages = owner_grads(enc_grad + [embed_pair], 2)
    links.unload()

    def own_chunk(value):
        if rows_high > 1:
            value = value[:, :, : D // 2].reshape(value.shape[0], width, rows_high, chunk)
            value = lax.psum_scatter(value, "rh", scatter_dimension=2, tiled=True)
            value = value.reshape(value.shape[0], width, chunk)
        return value

    enc_rows = to_rows(jnp.stack([o[0] for o in enc_feed]))
    enc_flat = flatten(enc_rows, spread, hid, period_groups)
    early_red = own_chunk(early_stages[-1])
    dec_red, cross_red = own_chunk(dec_stages[-1]), own_chunk(cross_stages[-1])
    square_local = functools.reduce(
        jnp.add, [jnp.sum(v * v) for v in (early_red, dec_red, cross_red, enc_rows, dec_rows)]
    )
    lane = jnp.arange(WIDE)
    extra = jnp.where(lane == 0, square_local, 0.0) + jnp.where(lane == 1, loss_local, 0.0)
    gain_local = jnp.stack(
        [gain_zero, gain_one, gain_two, gain_three, gain_four, gain_five, gain_six, extra]
    )
    gain_local = anchor(gain_local, enc_flat, dec_flat)
    everything = links.total(gain_local, rows_high)
    loss = everything[7, 1]
    grad_norm = jnp.sqrt(everything[7, 0] + jnp.sum(everything[:7] * everything[:7]))
    count = step_count[0].astype(F32)
    scalars = jnp.stack([1.0 / (1.0 - BETA_FIRST**count), 1.0 / (1.0 - BETA_SECOND**count)])
    slot_total = tokens * cols_n

    def attn_turn(value):
        return value.transpose(0, 1, 3, 2).reshape(12, width, chunk)

    def attn_return(value):
        return value.reshape(3, 4, width, chunk).transpose(0, 1, 3, 2)

    def table_turn(value):
        return value.transpose(0, 2, 1)

    new = finish(
        (slot_total / (3.0 * INNER)) ** 0.5,
        scalars,
        everything,
        (enc_flat, dec_flat),
        (early_red, dec_red, cross_red, join_features(everything[:7])),
        tuple(v.reshape(flat_shape) for v in (feed_weights, feed_first, feed_second)),
        tuple(attn_turn(v) for v in (attn_weights, attn_first, attn_second)),
        tuple(table_turn(v) for v in (table_weights, table_first, table_second)),
        (norm_gain_stack, gain_first, gain_second),
    )
    return (
        (loss, grad_norm)
        + tuple(attn_return(v) for v in new[3:6])
        + tuple(v.reshape(feed_weights.shape) for v in new[:3])
        + tuple(table_turn(v) for v in new[6:9])
        + tuple(new[9:])
    )


def solution(mesh):
    rows_high = mesh.shape["row"] // 2
    groups = mesh.shape["col"] // 4
    split = Mesh(mesh.devices.reshape(rows_high, 2, groups, 2, 2), ("rh", "c", "z", "y", "x"))
    row, col = ("rh", "c"), ("z", "y", "x")
    attn = P(None, None, row, col)
    feed = P(None, None, col, row)
    table = P(None, row, col)
    ids = P(row, col)
    in_specs = (ids,) * 4 + (P(row),) * 3 + (P(),) + (attn,) * 3 + (feed,) * 3 + (table,) * 3 + (P(),) * 3
    out_specs = (P(), P()) + (attn,) * 3 + (feed,) * 3 + (table,) * 3 + (P(),) * 3
    return jax.shard_map(
        functools.partial(step, (rows_high, groups)),
        mesh=split,
        in_specs=in_specs,
        out_specs=out_specs,
        check_vma=False,
    )
```
